32 devices in a mesh: aa: 8 (over y, x, core), ba: 4 (over z).
Axes of the slice: x: 2, y: 2, z: 4, core: 2. Of those that a mesh axis runs over, the one named last changes fastest.
Arguments:
- fast_query: bfloat16 [2, 2048, 5120], P(None, 'aa', 'ba'), may hold values from -6 to 6
- fast_key: bfloat16 [2, 2048, 5120], P(None, 'aa', 'ba'), may hold values from -6 to 6
- fast_value: bfloat16 [2, 2048, 5120], P(None, 'aa', 'ba'), may hold values from -6 to 6
- rates: float32 [2, 2048, 24], P(None, 'aa', 'ba'), may hold values from 5e-05 to 0.0005
- attn_query: bfloat16 [2, 2048, 5120], P(None, 'aa', 'ba'), may hold values from -4.5 to 4.5
- attn_key: bfloat16 [2, 2048, 5120], P(None, 'aa', 'ba'), may hold values from -4.5 to 4.5
- attn_value: bfloat16 [2, 2048, 5120], P(None, 'aa', 'ba'), may hold values from -6 to 6
- fast_weights: float32 [640, 3, 8, 640], P('aa', None, 'ba'), may hold values from -0.2814427 to 0.2814427
- gain: float32 [5120], replicated, may hold values from 0.5 to 1.5
Outputs:
- mixed: bfloat16 [2, 2048, 5120], P(None, ('aa', 'ba'))
- weights_out: float32 [640, 3, 8, 640], P('aa', None, 'ba')
- moment_out: float32 [640, 3, 8, 640], P('aa', None, 'ba')
The draws below stay inside these ranges and needn't reach their ends.
All inputs are finite; a program needn't handle non-finite values.
Results may differ from the reference program's by a relative error of at most 0.028.
Values may be sent and summed in bfloat16 or wider, within the bound.
A program may use at most 192 MiB of HBM per device.

```python
import math
import jax
import jax.numpy as jnp
from jax import lax

H = 8
DH = 640
FH = 640
AH = 40
AD = 128
WINDOW = 512
STRETCHES = 2
TOK_DEV = 256
TOKENS = 2048
N_AA = 8


def attention_pair(key):
    base = jax.random.fold_in(key, 7)
    key_q, key_k = jax.random.split(base, 2)
    shape = (STRETCHES, TOKENS, AH * AD)
    query = jnp.clip(jax.random.normal(key_q, shape, jnp.float32), -4.5, 4.5)
    keys = jnp.clip(jax.random.normal(key_k, shape, jnp.float32), -4.5, 4.5)
    return (query, keys)


def draw_attn_query(key, part):
    query, keys = attention_pair(key)
    return query.astype(jnp.bfloat16)


def draw_attn_key(key, part):
    query, keys = attention_pair(key)
    return keys.astype(jnp.bfloat16)


def draw_fast_weights(key, part):
    key_b, key_c = jax.random.split(jax.random.fold_in(key, 11), 2)
    shape = (FH, 3, H, DH)
    base = jnp.clip(jax.random.normal(key_b, shape, jnp.float32), -4.0, 4.0)
    cols = jnp.exp(jax.random.uniform(key_c, (3, H, DH), jnp.float32, 0.0, math.log(10.0)))
    return base * cols[None] * (8.0 / (45.0 * math.sqrt(DH)))


def levels(rng, shape, shards, least, top_value):
    factor_of = 1.0
    for position, parts in shards:
        steps = jax.random.uniform(jax.random.fold_in(jax.random.fold_in(rng, 6), position), (parts,), jnp.float32, least / len(shards), top_value / len(shards))
        factor_of = factor_of * jnp.repeat(jnp.exp(steps), shape[position] // parts).reshape((-1,) + (1,) * (len(shape) - 1 - position))
    return factor_of


def bell_draw(key, dims, scale, most, shards=(), held_as=jnp.bfloat16):
    values = scale * jax.random.normal(key, dims, jnp.float32)
    if shards:
        values = values * levels(key, dims, shards, -0.22, 0.18)
    return jnp.clip(values, -most, most).astype(held_as)


def setup_inputs(seed: int = 0) -> dict:
    splits = jax.random.split(jax.random.key(seed), 10)
    fast_query = bell_draw(splits[0], (STRETCHES, TOKENS, H * DH), 1.0, 6.0, ((1, 8), (2, 4)))
    fast_key = bell_draw(splits[1], (STRETCHES, TOKENS, H * DH), 1.0, 6.0, ((1, 8), (2, 4)))
    fast_value = bell_draw(splits[2], (STRETCHES, TOKENS, H * DH), 1.0, 6.0, ((1, 8), (2, 4)))
    rates = jnp.clip(jnp.exp(math.log(0.0005) - 2.3025852 * jax.random.uniform(splits[3], (STRETCHES, TOKENS, 3 * H), jnp.float32) ** levels(splits[3], (STRETCHES, TOKENS, 3 * H), ((1, 8), (2, 4)), -0.2, 0.2)), 4.999999873689376e-05, 0.0005)
    attn_query = draw_attn_query(jax.random.fold_in(splits[9], 71), 0)
    attn_key = draw_attn_key(jax.random.fold_in(splits[9], 71), 0)
    attn_value = bell_draw(splits[6], (STRETCHES, TOKENS, AH * AD), 1.0, 6.0, ((1, 8), (2, 4)))
    fast_weights = draw_fast_weights(jax.random.fold_in(splits[9], 71), 0)
    gain = jnp.clip(1.0 + 0.1 * jax.random.normal(splits[8], (H * DH,), jnp.float32), 0.5, 1.5)
    return {"fast_query": fast_query, "fast_key": fast_key, "fast_value": fast_value, "rates": rates, "attn_query": attn_query, "attn_key": attn_key, "attn_value": attn_value, "fast_weights": fast_weights, "gain": gain}


BETA = 0.9
EPS = 1e-06

def activation(x):
    sig = jax.nn.sigmoid(x)
    return (x * sig, sig * (1.0 + x * (1.0 - sig)))

def project(x, w):
    return jnp.einsum('nhd,fhd->nhf', x.astype(jnp.float32), w.astype(jnp.float32))

def fast_stretch(weights, query, key, value, rate):
    tokens = query.shape[0]
    wbf = weights.astype(jnp.bfloat16)
    q = query.reshape(tokens, H, DH)
    k = key.reshape(tokens, H, DH)
    v = value.reshape(tokens, H, DH)
    act_q, slope_q = activation(project(q, wbf[:, 0]))
    hidden_q = (act_q * project(q, wbf[:, 1])).astype(jnp.bfloat16)
    out = jnp.einsum('nhf,fhd->nhd', hidden_q.astype(jnp.float32), wbf[:, 2].astype(jnp.float32)).reshape(tokens, H * DH)
    gate_in = project(k, wbf[:, 0])
    up_in = project(k, wbf[:, 1])
    back_in = project(v, wbf[:, 2])
    act, slope = activation(gate_in)
    rate = rate.reshape(tokens, H, 3)
    gate_x = (rate[..., 0:1] * (-back_in * up_in * slope)).astype(jnp.bfloat16)
    up_x = (rate[..., 1:2] * (-back_in * act)).astype(jnp.bfloat16)
    down_x = (rate[..., 2:3] * -(act * up_in)).astype(jnp.bfloat16)

    def block(total, index):
        start = index * TOK_DEV

        def cut(x):
            return lax.dynamic_slice_in_dim(x, start, TOK_DEV, 0).astype(jnp.float32)
        gate_g = jnp.einsum('nhf,nhd->fhd', cut(gate_x), cut(k))
        up_g = jnp.einsum('nhf,nhd->fhd', cut(up_x), cut(k))
        down_g = jnp.einsum('nhf,nhd->fhd', cut(down_x), cut(v))
        stacked = jnp.stack([gate_g, up_g, down_g], 1)
        rounded = lax.optimization_barrier(stacked.astype(jnp.bfloat16))
        return (total + rounded.astype(jnp.float32), None)
    grads, unused = lax.scan(block, jnp.zeros((FH, 3, H, DH), jnp.float32), jnp.arange(N_AA, dtype=jnp.int32))
    return (out, grads)

def renorm(trial, target):
    return trial * (target / jnp.sqrt(lax.optimization_barrier(jnp.sum(trial * trial, 0)) + EPS))

def attend(query, key, value):
    total = STRETCHES * TOKENS
    q = query.reshape(total, AH, AD)
    k = key.reshape(total, AH, AD)
    v = value.reshape(total, AH, AD)
    reach = (WINDOW - 2) // TOK_DEV + 1
    margin = reach * TOK_DEV
    k_pad = jnp.concatenate([jnp.zeros((margin, AH, AD), k.dtype), k], 0)
    v_pad = jnp.concatenate([jnp.zeros((margin, AH, AD), v.dtype), v], 0)

    def block(index):
        start = index * TOK_DEV
        q_blk = lax.dynamic_slice_in_dim(q, start, TOK_DEV, 0).astype(jnp.float32)
        k_blk = lax.dynamic_slice_in_dim(k_pad, start, margin + TOK_DEV, 0).astype(jnp.float32)
        v_blk = lax.dynamic_slice_in_dim(v_pad, start, margin + TOK_DEV, 0).astype(jnp.float32)
        scores = jnp.einsum('qhe,khe->hqk', q_blk, k_blk) / math.sqrt(AD)
        q_pos = start + jnp.arange(TOK_DEV, dtype=jnp.int32)
        k_pos = start - margin + jnp.arange(margin + TOK_DEV, dtype=jnp.int32)
        mask = (k_pos[None, :] <= q_pos[:, None]) & (k_pos[None, :] > q_pos[:, None] - WINDOW) & (k_pos[None, :] >= 0)
        scores = jnp.where(mask[None], scores, -1e+30)
        top = lax.optimization_barrier(jnp.max(scores, -1, keepdims=True))
        probs = jnp.exp(scores - top)
        denom = lax.optimization_barrier(jnp.sum(probs, -1))
        rounded = lax.optimization_barrier(probs.astype(jnp.bfloat16)).astype(jnp.float32)
        out = jnp.einsum('hqk,khe->qhe', rounded, v_blk)
        return out / jnp.transpose(denom)[:, :, None]
    outs = lax.map(block, jnp.arange(total // TOK_DEV, dtype=jnp.int32))
    return outs.reshape(STRETCHES, TOKENS, AH * AD)

def reference(fast_query, fast_key, fast_value, rates, attn_query, attn_key, attn_value, fast_weights, gain):
    target = jnp.sqrt(lax.optimization_barrier(jnp.sum(fast_weights * fast_weights, 0)) + EPS)
    weights = fast_weights
    moment = jnp.zeros_like(fast_weights)
    fast_out = []
    for stretch in range(STRETCHES):
        out, grads = fast_stretch(weights, fast_query[stretch], fast_key[stretch], fast_value[stretch], rates[stretch])
        fast_out.append(out)
        moment = BETA * moment + grads
        weights = renorm(weights - moment, target)
    attention = attend(attn_query, attn_key, attn_value)
    combined = lax.optimization_barrier((jnp.stack(fast_out) + attention).astype(jnp.bfloat16)).astype(jnp.float32)
    scale = lax.rsqrt(lax.optimization_barrier(jnp.mean(combined * combined, -1, keepdims=True)) + EPS)
    mixed = (combined * scale * gain).astype(jnp.bfloat16)
    return (mixed, weights, moment)
```

```python
import functools
import math

import jax
import jax.numpy as jnp
from jax import lax
from jax.experimental import pallas as pl
from jax.experimental.pallas import tpu as pltpu
from jax.sharding import PartitionSpec as P

AD = 128
WINDOW = 512


BETA = 0.9
EPS = 1e-06


def shift(x, axis, by):
    length = lax.axis_size(axis)
    return lax.ppermute(x, axis, [(i, (i + by) % length) for i in range(length)])


def activation(x):
    sig = jax.nn.sigmoid(x)
    return (x * sig, sig * (1.0 + x * (1.0 - sig)))


def project(x, w):
    return jnp.einsum("nhd,hfd->nhf", x, w, preferred_element_type=jnp.float32)


def forward(w, query):
    rows, heads = query.shape[0], w.shape[1]
    q = query.reshape(rows, heads, -1)
    act_q, _ = activation(project(q, w[0]))
    hidden_q = (act_q * project(q, w[1])).astype(jnp.bfloat16)
    return jnp.einsum("nhf,hfd->nhd", hidden_q, w[2], preferred_element_type=jnp.float32).reshape(
        rows, -1
    )


def partial_grads(w, key, value, rate):
    rows, heads = key.shape[0], w.shape[1]
    k = key.reshape(rows, heads, -1)
    v = value.reshape(rows, heads, -1)
    gate_in = project(k, w[0])
    up_in = project(k, w[1])
    back_in = project(v, w[2])
    act, slope = activation(gate_in)
    gate_x = (rate[..., 0:1] * (-back_in * up_in * slope)).astype(jnp.bfloat16)
    up_x = (rate[..., 1:2] * (-back_in * act)).astype(jnp.bfloat16)
    down_x = (rate[..., 2:3] * -(act * up_in)).astype(jnp.bfloat16)

    def part(left, right):
        return jnp.einsum("nhf,nhd->hfd", left, right, preferred_element_type=jnp.float32)

    return jnp.stack([part(gate_x, k), part(up_x, k), part(down_x, v)]).astype(jnp.bfloat16)


def attend_kernel(rows, groups, q_ref, *refs):
    out_ref = refs[-1]
    stretch = pl.program_id(0)
    base = stretch * (rows * groups) + lax.axis_index("aa") * rows
    q = q_ref[0]
    scores = []
    blocks = (len(refs) - 1) // 2
    row = lax.broadcasted_iota(jnp.int32, (rows, rows), 0)
    col = lax.broadcasted_iota(jnp.int32, (rows, rows), 1)
    for back in range(blocks):
        s = lax.dot_general(
            q, refs[back][0], (((1,), (1,)), ((), ())), preferred_element_type=jnp.float32
        ) / math.sqrt(AD)
        gap = row - col + back * rows
        ok = (gap >= 0) & (gap < WINDOW) & (col >= back * rows - base)
        scores.append(jnp.where(ok, s, -1e30))
    top = functools.reduce(jnp.maximum, [jnp.max(s, -1, keepdims=True) for s in scores])
    total = 0.0
    acc = 0.0
    for back in range(blocks):
        p = jnp.exp(scores[back] - top)
        total = total + jnp.sum(p, -1, keepdims=True)
        acc = acc + jnp.dot(
            p.astype(jnp.bfloat16), refs[blocks + back][0], preferred_element_type=jnp.float32
        )
    out_ref[0] = acc / total


def attend(q, keys, values):
    stretches, rows, width = q.shape
    groups = lax.axis_size("aa")
    own = pl.BlockSpec((1, rows, AD), lambda s, h: (s, 0, h))
    index = lax.axis_index("aa")

    def moved(x, back):
        if not back:
            return x
        return jnp.where(index < back, jnp.concatenate([x[:1], x[:-1]], 0), x)

    keys = [moved(x, b) for b, x in enumerate(keys)]
    values = [moved(x, b) for b, x in enumerate(values)]
    return pl.pallas_call(
        functools.partial(attend_kernel, rows, groups),
        grid=(stretches, width // AD),
        in_specs=[own] * (1 + 2 * len(keys)),
        out_specs=own,
        out_shape=jax.ShapeDtypeStruct(q.shape, jnp.float32),
        cost_estimate=pl.CostEstimate(
            flops=4 * stretches * rows * rows * len(keys) * width,
            bytes_accessed=40 * q.size,
            transcendentals=stretches * rows * rows * len(keys) * width // AD,
        ),
        name="attend",
    )(q, *keys, *values)


def sum_kernel(n, x_ref, out_ref, land, send_sem, recv_sem):
    me = lax.axis_index("aa")
    barrier = pltpu.get_barrier_semaphore()
    for step in range(1, n):
        pl.semaphore_signal(
            barrier,
            inc=1,
            device_id={"aa": lax.rem(me + step, n)},
            device_id_type=pl.DeviceIdType.MESH,
        )
    pl.semaphore_wait(barrier, n - 1)
    copies = []
    for step in range(1, n):
        copy = pltpu.make_async_remote_copy(
            src_ref=x_ref,
            dst_ref=land.at[step],
            send_sem=send_sem.at[step],
            recv_sem=recv_sem.at[step],
            device_id={"aa": lax.rem(me + step, n)},
            device_id_type=pl.DeviceIdType.MESH,
        )
        copy.start()
        copies.append(copy)
    total = x_ref[...]
    for step in range(1, n):
        copies[step - 1].wait_recv()
        total = total + land[step]
    for copy in copies:
        copy.wait_send()
    out_ref[...] = total


def sum_over(x):
    n = lax.axis_size("aa")
    vmem = pl.BlockSpec(memory_space=pltpu.VMEM)
    return pl.pallas_call(
        functools.partial(sum_kernel, n),
        in_specs=[vmem],
        out_specs=vmem,
        out_shape=jax.ShapeDtypeStruct(x.shape, x.dtype),
        scratch_shapes=[
            pltpu.VMEM((n,) + x.shape, x.dtype),
            pltpu.SemaphoreType.DMA((n,)),
            pltpu.SemaphoreType.DMA((n,)),
        ],
        compiler_params=pltpu.CompilerParams(collective_id=1, has_side_effects=True),
        name="sum_over",
    )(x)


def tie(values, anchor):
    out = lax.optimization_barrier(tuple(values) + (anchor,))
    return out[:-1], out[-1]


def local(
    fast_query, fast_key, fast_value, rates, attn_query, attn_key, attn_value, fast_weights, gain
):
    stretches, rows, width = fast_query.shape
    local_rows = fast_weights.shape[0]
    heads = fast_weights.shape[2]
    rate = rates.reshape(stretches, rows, heads, 3)
    index = lax.axis_index("aa")
    groups = lax.axis_size("aa")
    first_row = index * local_rows

    shard = jnp.transpose(fast_weights, (1, 2, 0, 3))
    wb = lax.all_gather(shard.astype(jnp.bfloat16), "aa", axis=2, tiled=True)
    (attn_key, attn_value), wb = tie((attn_key, attn_value), wb)
    far = [shift(attn_key, "aa", 2), shift(attn_value, "aa", 2)]

    full = wb.astype(jnp.float32)
    target = jnp.sqrt(jnp.sum(full * full, 2, keepdims=True) + EPS)
    gp = partial_grads(wb, fast_key[0], fast_value[0], rate[0])
    grads = lax.psum(gp, "aa").astype(jnp.float32)

    (fq,), _ = tie((fast_query,), gp)
    out0 = forward(wb, fq[0])
    far, out0 = tie(far, out0)
    odd = index % 2 == 1
    swap = [(i, i ^ 1) for i in range(groups)]
    near = [
        lax.ppermute(jnp.where(odd, f, o), "aa", swap) for f, o in zip(far, (attn_key, attn_value))
    ]
    attention = attend(
        attn_query, [attn_key, near[0], far[0]], [attn_value, near[1], far[1]]
    )
    (attention,), grads = tie((attention,), grads)

    trial = full - grads
    updated = trial * (target / jnp.sqrt(jnp.sum(trial * trial, 2, keepdims=True) + EPS))
    ub = updated.astype(jnp.bfloat16)
    gp1 = partial_grads(ub, fast_key[1], fast_value[1], rate[1])
    grads1 = lax.psum_scatter(gp1, "aa", scatter_dimension=2, tiled=True).astype(jnp.float32)
    (fq1,), _ = tie((fast_query,), gp1)
    out1 = forward(ub, fq1[1])
    combined = (jnp.stack([out0, out1]) + attention).astype(jnp.bfloat16)

    moment = BETA * lax.dynamic_slice_in_dim(grads, first_row, local_rows, 2) + grads1
    own = lax.dynamic_slice_in_dim(updated, first_row, local_rows, 2)
    trial = own - moment
    squares = sum_over(jnp.sum(trial * trial, 2).reshape(-1, trial.shape[3]))
    squares = squares.reshape(trial.shape[:2] + (1, trial.shape[3]))
    weights = trial * (target / jnp.sqrt(squares + EPS))

    arrived = lax.all_to_all(combined, "ba", split_axis=1, concat_axis=2, tiled=True)
    values = arrived.astype(jnp.float32)
    scale = lax.rsqrt(jnp.mean(values * values, -1, keepdims=True) + EPS)
    mixed = (values * scale * gain).astype(jnp.bfloat16)
    back = (2, 0, 1, 3)
    return (mixed, jnp.transpose(weights, back), jnp.transpose(moment, back))


class Comm:
    def __init__(self, send, recv):
        self.send, self.recv, self.used = send, recv, 0

    def slots(self, count):
        first = self.used
        self.used += count
        return first

    def make(self, slot, src, dst, peer, lands=None):
        return pltpu.make_async_remote_copy(
            src_ref=src,
            dst_ref=dst,
            send_sem=self.send.at[slot],
            recv_sem=self.recv.at[slot if lands is None else lands],
            device_id=peer,
            device_id_type=pl.DeviceIdType.MESH,
        )


NT = (((1,), (1,)), ((), ()))
TN = (((0,), (0,)), ((), ()))
NN = (((1,), (0,)), ((), ()))


def block_kernel(
    n,
    parts,
    fq,
    fk,
    fv,
    rate,
    aq,
    ak,
    av,
    shard,
    gain,
    mixed,
    weights,
    moment,
    first,
    second,
    gp,
    pair,
    sums,
    landed,
    last_sums,
    last_landed,
    kb,
    vb,
    qb,
    xs,
    rate_rows,
    rate_far,
    aqb,
    akb,
    avb,
    far,
    near,
    relay,
    fast,
    back,
    comb,
    land,
    past,
    held_w,
    goal,
    goal_far,
    w_far,
    m_out,
    m_far,
    sq,
    loads,
    send,
    recv,
):
    me = lax.axis_index("aa")
    mine = lax.axis_index("ba")
    group, core = me // 2, lax.rem(me, 2)
    teams = n // 2
    _, _, r, depth = shard.shape
    stretches, rows, width = fq.shape
    row_at, col_at = group // 2, lax.rem(group, 2)
    other = 1 - row_at
    beside = row_at * 2 + 1 - col_at
    above = other * 2 + col_at
    across = other * 2 + 1 - col_at
    partner = {"aa": group * 2 + 1 - core}
    to_x = {"aa": beside * 2 + core}
    to_y = {"aa": above * 2 + core}
    comm = Comm(send, recv)
    bf, f32 = jnp.bfloat16, jnp.float32
    tail = []

    def cols_of(h):
        return pl.ds(pl.multiple_of(h * depth, AD), depth)

    def slot_of(g):
        return core * teams + g

    def mm(a, b, dims):
        return lax.dot_general(a, b, dims, preferred_element_type=f32)

    def run(*args):
        copy = comm.make(comm.slots(1), *args)
        copy.start()
        tail.append(copy)
        return copy

    def drained(copy):
        copy.wait_send()
        tail[:] = [c for c in tail if c is not copy]

    barrier = pltpu.get_barrier_semaphore()
    for step in range(1, n):
        pl.semaphore_signal(
            barrier,
            inc=1,
            device_id={"aa": lax.rem(me + step, n)},
            device_id_type=pl.DeviceIdType.MESH,
        )
    for step in range(1, parts):
        pl.semaphore_signal(
            barrier,
            inc=1,
            device_id={"ba": lax.rem(mine + step, parts)},
            device_id_type=pl.DeviceIdType.MESH,
        )

    local = {}

    def load(name, src, dst):
        copy = pltpu.make_async_copy(src, dst, loads.at[len(local)])
        copy.start()
        local[name] = copy

    own_rows, far_rows = pl.ds(0, rows), pl.ds(rows, rows)
    tokens = {"k": (fk, kb), "v": (fv, vb), "q": (fq, qb)}
    for s in range(stretches):
        for name, (src, dst) in tokens.items():
            load((name, s), src.at[s, :, cols_of(row_at)], dst.at[s, own_rows])
    for name, src, dst in (("aq", aq, aqb), ("ak", ak, akb), ("av", av, avb)):
        load(name, src, dst)
    pl.semaphore_wait(barrier, n + parts - 2)

    sent = {}

    def send_tokens(name, s):
        src, dst = tokens[name]
        sent[name, s] = run(src.at[s, :, cols_of(other)], dst.at[s, far_rows], to_y)

    held = (ak, av)
    held_here = (akb, avb)
    final = comm.slots(2 * stretches)
    relays = comm.slots(stretches)
    swaps = comm.slots(2 * stretches)

    def halo_copy(t, s, direct):
        slot = final + t * stretches + s
        if direct:
            return comm.make(slot, held[t].at[s], far.at[t, s], to_x)
        return comm.make(slot, held[t].at[s], relay.at[s], (to_x, to_y)[t], relays + s)

    def relay_copy(t, s):
        slot = final + t * stretches + s
        return comm.make(relays + s, relay.at[s], far.at[t, s], (to_y, to_x)[t], slot)

    def sends_far(s):
        return (col_at == 1) & ((group < teams - 1) | (s < stretches - 1))

    def relays_far(s):
        return (s < stretches - 1) | (group == 0) | (group == teams - 1)

    def receives(s):
        return (s < stretches - 1) | (group > 0)

    def halo(s):
        for t in range(2):

            @pl.when(col_at == 0)
            def _():
                halo_copy(t, s, True).start()

            @pl.when(sends_far(s))
            def _():
                halo_copy(t, s, False).start()

    def halo_relay(s):
        for t in range(2):

            @pl.when((col_at == t) & relays_far(s))
            def _():
                halo_copy(0, s, False).wait_recv()
                relay_copy(t, s).start()

    def halo_swap(s):
        for t in range(2):
            slot = swaps + t * stretches + s
            onward = comm.make(slot, far.at[t, s], near.at[t, s], partner)
            inward = comm.make(slot, held_here[t].at[s], near.at[t, s], partner)

            @pl.when(core == 0)
            def _():
                inward.start()

            @pl.when(receives(s))
            def _():
                halo_copy(t, s, True).wait_recv()

            @pl.when((core == 1) & receives(s))
            def _():
                onward.start()

        for t in range(2):
            slot = swaps + t * stretches + s
            copy = comm.make(slot, held_here[t].at[s], near.at[t, s], partner)

            @pl.when((core == 1) | receives(s))
            def _():
                copy.wait_recv()

            @pl.when((core == 0) | receives(s))
            def _():
                copy.wait_send()

    def halo_sent(s):
        for t in range(2):

            @pl.when((col_at == 0) | sends_far(s))
            def _():
                halo_copy(t, s, True).wait_send()

        @pl.when(relays_far(s))
        def _():
            relay_copy(0, s).wait_send()

    def whole(ref, m):
        return ref[m].reshape(n * r, depth)

    def columns_of(ref):
        rate_rows[...] = jnp.zeros_like(rate_rows)
        for s in range(stretches):
            for m in range(3):
                rate_rows[s, pl.ds(m, 1), :] = ref[m, pl.ds(s, 1), :]
        return [jnp.transpose(rate_rows[s]) for s in range(stretches)]

    def hidden(ref, s, part, rates):
        at = far_rows if part else own_rows
        k, v = kb[s, at], vb[s, at]
        gate_in = mm(k, whole(ref, 0), NT)
        up_in = mm(k, whole(ref, 1), NT)
        back_in = mm(v, whole(ref, 2), NT)
        act, slope = activation(gate_in)
        xs[0, at] = (rates[:, 0:1] * (-back_in * up_in * slope)).astype(bf)
        xs[1, at] = (rates[:, 1:2] * (-back_in * act)).astype(bf)
        xs[2, at] = (rates[:, 2:3] * -(act * up_in)).astype(bf)

    def grads(phase):
        copies = []
        for m in range(3):
            other_side = vb[phase] if m == 2 else kb[phase]
            gp[m] = mm(xs[m], other_side, TN).astype(bf).reshape(n, r, depth)
            copies.append(
                run(gp.at[m, pl.ds((1 - core) * teams, teams)], pair.at[phase, m], partner)
            )
        return copies

    def both(phase, m, g):
        return gp[m, slot_of(g)].astype(f32) + pair[phase, m, g].astype(f32)

    def forward(ref, s, part):
        q = qb[s, far_rows if part else own_rows]
        act, _ = activation(mm(q, whole(ref, 0), NT))
        inner = (act * mm(q, whole(ref, 1), NT)).astype(bf)
        out = mm(inner, whole(ref, 2), NN).astype(bf)
        if not part:
            fast[s, :, cols_of(row_at)] = out
            return None
        back[s] = out
        return run(back.at[s], fast.at[s, :, cols_of(row_at)], to_y)

    def attention(s):
        base = s * (rows * n) + me * rows
        places = [s] + [jnp.where(me < b, max(s - 1, 0), s) for b in (1, 2)]
        row = lax.broadcasted_iota(jnp.int32, (rows, rows), 0)
        col = lax.broadcasted_iota(jnp.int32, (rows, rows), 1)
        oks = []
        for behind in range(3):
            gap = row - col + behind * rows
            oks.append((gap >= 0) & (gap < WINDOW) & (col >= behind * rows - base))

        @pl.loop(0, width // AD)
        def _(h):
            cols = pl.ds(pl.multiple_of(h * AD, AD), AD)
            keys = [akb[s, :, cols], near[0, places[1], :, cols], far[0, places[2], :, cols]]
            values = [avb[s, :, cols], near[1, places[1], :, cols], far[1, places[2], :, cols]]
            q = aqb[s, :, cols]
            scores = [
                jnp.where(ok, mm(q, k, NT) / math.sqrt(AD), -1e30) for ok, k in zip(oks, keys)
            ]
            top = functools.reduce(
                jnp.maximum, [jnp.max(x, -1, keepdims=True) for x in scores]
            )
            total, out = 0.0, 0.0
            for x, v in zip(scores, values):
                p = jnp.exp(x - top)
                total = total + jnp.sum(p, -1, keepdims=True)
                out = out + mm(p.astype(bf), v, NN)
            comb[s, :, cols] = (fast[s, :, cols].astype(f32) + out / total).astype(bf)

    def exchange(s):
        first_slot = comm.slots(parts)
        chunk = rows // parts
        copies = []
        for step in range(1, parts):
            z = lax.rem(mine + step, parts)
            take = pl.ds(pl.multiple_of(z * chunk, chunk), chunk)
            copy = comm.make(
                first_slot + step, comb.at[s, take], land.at[s, step], {"ba": z}
            )
            copy.start()
            copies.append(copy)
        return copies

    def finish(s, copies):
        chunk = rows // parts
        take = pl.ds(pl.multiple_of(mine * chunk, chunk), chunk)
        land[s, 0] = comb[s, take]
        for copy in copies:
            copy.wait()
        squares = 0.0
        for step in range(parts):
            x = land[s, step].astype(f32)
            squares = squares + jnp.sum(x * x, -1, keepdims=True)
        scale = lax.rsqrt(squares / (parts * width) + EPS)
        for step in range(parts):
            z = lax.rem(mine + parts - step, parts)
            cols = pl.ds(pl.multiple_of(z * width, 128), width)
            x = land[s, step].astype(f32)
            mixed[s, :, cols] = (x * scale * gain[:, cols]).astype(bf)

    def renorm(m):
        before, after = 0.0, 0.0
        for j in range(n):
            w = first[m, j].astype(f32)
            t = w - second[m, j].astype(f32)
            before = before + jnp.sum(w * w, 0, keepdims=True)
            after = after + jnp.sum(t * t, 0, keepdims=True)
        target = jnp.sqrt(before + EPS)
        goal[m] = target
        ratio = target / jnp.sqrt(after + EPS)
        for b, g in enumerate((group, above)):
            grad = second[m, slot_of(g)].astype(f32)
            past[b, m] = BETA * grad
            held_w[b, m] = (first[m, slot_of(g)].astype(f32) - grad) * ratio
        for j in range(n):
            w = first[m, j].astype(f32)
            t = w - second[m, j].astype(f32)
            second[m, j] = (t * ratio).astype(bf)

    here, near_y, near_x = slot_of(group), slot_of(above), slot_of(beside)
    corner = slot_of(across)
    up = run(shard.at[other], first.at[:, here], to_y)
    side = run(shard.at[row_at], first.at[:, here], to_x)
    twins = [run(shard.at[row_at], first.at[:, here], partner)]
    rate_copy = run(rate.at[pl.ds(3 * other, 3)], rate_far, to_y)
    first[:, here] = shard[row_at]
    rates = columns_of(rate.at[pl.ds(3 * row_at, 3)])
    up.wait_recv()
    onward = run(first.at[:, near_y], first.at[:, near_y], to_x)
    twins.append(run(first.at[:, near_y], first.at[:, near_y], partner))
    send_tokens("k", 0)
    send_tokens("v", 0)
    side.wait_recv()
    twins.append(run(first.at[:, near_x], first.at[:, near_x], partner))
    halo(0)
    onward.wait_recv()
    twins.append(run(first.at[:, corner], first.at[:, corner], partner))
    for copy in twins:
        copy.wait_recv()

    local["k", 0].wait()
    local["v", 0].wait()
    hidden(first, 0, 0, rates[0])
    rate_copy.wait_recv()
    far_rates = columns_of(rate_far)
    sent["k", 0].wait_recv()
    sent["v", 0].wait_recv()
    for name, s in (("q", 0), ("k", 1), ("v", 1), ("q", 1)):
        send_tokens(name, s)
    hidden(first, 0, 1, far_rates[0])
    pairs = grads(0)
    crossing = []
    for m in range(3):
        pairs[m].wait_recv()
        for g in range(teams):
            sums[m, g] = both(0, m, g).astype(bf)
        crossing.append(run(sums.at[m], landed.at[m], to_x))
    sent["q", 0].wait_recv()
    arriving = forward(first, 0, 1)
    local["q", 0].wait()
    forward(first, 0, 0)
    halo_relay(0)
    for name in ("aq", "ak", "av"):
        local[name].wait()
    halo_swap(0)
    arriving.wait_recv()
    attention(0)
    mixing0 = exchange(0)
    half = pl.ds(core * teams, teams)
    twins = []
    for m in range(3):
        crossing[m].wait_recv()
        second[m, half] = (sums[m].astype(f32) + landed[m].astype(f32)).astype(bf)
        twins.append(run(second.at[m, half], second.at[m, half], partner))
    halo(1)
    for m in range(3):
        twins[m].wait_recv()
        drained(twins[m])
        drained(pairs[m])
        renorm(m)
    w_copy = run(second.at[:, near_y], w_far, to_y)
    goal_copy = run(goal, goal_far, to_y)
    for name in "kv":
        local[name, 1].wait()
        sent[name, 1].wait_recv()
    hidden(second, 1, 0, rates[1])
    hidden(second, 1, 1, far_rates[1])
    pairs = grads(1)
    crossing = []
    for m in range(3):
        pairs[m].wait_recv()
        for k in range(2):
            last_sums[m, k] = both(1, m, k * 2 + 1 - col_at).astype(bf)
        crossing.append(run(last_sums.at[m], last_landed.at[m], to_x))
    sent["q", 1].wait_recv()
    arriving = forward(second, 1, 1)
    local["q", 1].wait()
    forward(second, 1, 0)
    halo_relay(1)
    finish(0, mixing0)
    halo_swap(1)
    arriving.wait_recv()
    attention(1)
    mixing1 = exchange(1)
    m_copies = []
    for m in range(3):
        crossing[m].wait_recv()
        squares = 0.0
        for b, (g, k) in enumerate(((group, row_at), (above, other))):
            momentum = past[b, m] + both(1, m, g) + last_landed[m, k].astype(f32)
            trial = held_w[b, m] - momentum
            squares = squares + jnp.sum(trial * trial, 0, keepdims=True)
            if b:
                m_out[m] = momentum.astype(bf)
            else:
                moment[row_at, m] = momentum
                weights[row_at, m] = trial
        m_copies.append(run(m_out.at[m], m_far.at[m], to_y))
        sq[me, m] = squares
    first_slot = comm.slots(n)
    copies = []
    for step in range(1, n):
        copy = comm.make(
            first_slot + step, sq.at[me], sq.at[me], {"aa": lax.rem(me + step, n)}
        )
        copy.start()
        copies.append(copy)
    finish(1, mixing1)
    for copy in copies:
        copy.wait()
    w_copy.wait_recv()
    goal_copy.wait_recv()
    for m in range(3):
        m_copies[m].wait_recv()
        squares, squares_far = 0.0, 0.0
        for j in range(teams):
            squares = squares + sq[row_at * teams + j, m]
            squares_far = squares_far + sq[other * teams + j, m]
        weights[row_at, m] = weights[row_at, m] * (goal[m] / jnp.sqrt(squares + EPS))
        momentum = m_far[m].astype(f32)
        moment[other, m] = momentum
        weights[other, m] = (w_far[m].astype(f32) - momentum) * (
            goal_far[m] / jnp.sqrt(squares_far + EPS)
        )
    for copy in tail:
        copy.wait_send()
    for s in range(stretches):
        halo_sent(s)


def run_blocks(fq, fk, fv, rates, aq, ak, av, shard, gain):
    n, parts = lax.axis_size("aa"), lax.axis_size("ba")
    stretches, rows, width = fq.shape
    heads, _, r, depth = shard.shape
    teams = n // 2
    vmem = pl.BlockSpec(memory_space=pltpu.VMEM)
    hbm = pl.BlockSpec(memory_space=pl.ANY)
    piece = (r, depth)
    bf, f32 = jnp.bfloat16, jnp.float32
    slots = 5 * stretches + 2 * parts + n + 64
    token = pltpu.VMEM((stretches, 2 * rows, depth), bf)
    features = pltpu.VMEM((stretches, rows, width), bf)
    return pl.pallas_call(
        functools.partial(block_kernel, n, parts),
        in_specs=[hbm] * 3 + [vmem] + [hbm] * 3 + [vmem] * 2,
        out_specs=(vmem,) * 3,
        out_shape=(
            jax.ShapeDtypeStruct((stretches, rows // parts, width * parts), bf),
            jax.ShapeDtypeStruct((heads, 3) + piece, f32),
            jax.ShapeDtypeStruct((heads, 3) + piece, f32),
        ),
        scratch_shapes=[
            pltpu.VMEM((3, n) + piece, bf),
            pltpu.VMEM((3, n) + piece, bf),
            pltpu.VMEM((3, n) + piece, bf),
            pltpu.VMEM((2, 3, teams) + piece, bf),
            pltpu.VMEM((3, teams) + piece, bf),
            pltpu.VMEM((3, teams) + piece, bf),
            pltpu.VMEM((3, 2) + piece, bf),
            pltpu.VMEM((3, 2) + piece, bf),
            token,
            token,
            token,
            pltpu.VMEM((3, 2 * rows, depth), bf),
            pltpu.VMEM((stretches, 8, rows), f32),
            pltpu.VMEM((3, stretches, rows), f32),
            features,
            features,
            features,
            pltpu.VMEM((2, stretches, rows, width), bf),
            pltpu.VMEM((2, stretches, rows, width), bf),
            features,
            features,
            pltpu.VMEM((stretches, rows, depth), bf),
            features,
            pltpu.VMEM((stretches, parts, rows // parts, width), bf),
            pltpu.VMEM((2, 3) + piece, f32),
            pltpu.VMEM((2, 3) + piece, f32),
            pltpu.VMEM((3, 1, depth), f32),
            pltpu.VMEM((3, 1, depth), f32),
            pltpu.VMEM((3,) + piece, bf),
            pltpu.VMEM((3,) + piece, bf),
            pltpu.VMEM((3,) + piece, bf),
            pltpu.VMEM((n, 3, 1, depth), f32),
            pltpu.SemaphoreType.DMA((3 * stretches + 3,)),
            pltpu.SemaphoreType.DMA((slots,)),
            pltpu.SemaphoreType.DMA((slots,)),
        ],
        compiler_params=pltpu.CompilerParams(
            collective_id=2, has_side_effects=True, vmem_limit_bytes=67043328
        ),
        name="blocks",
    )(fq, fk, fv, rates, aq, ak, av, shard, gain)


def local_blocks(fq, fk, fv, rates, aq, ak, av, fast_weights, gain):
    shard = jnp.transpose(fast_weights.astype(jnp.bfloat16), (2, 1, 0, 3))
    rate = jnp.transpose(rates, (2, 0, 1))
    mixed, weights, moment = run_blocks(fq, fk, fv, rate, aq, ak, av, shard, gain[None])
    back = (2, 1, 0, 3)
    return (mixed, jnp.transpose(weights, back), jnp.transpose(moment, back))


def pick(*args):
    stretches, rows, _ = args[0].shape
    r, _, heads, depth = args[7].shape
    n, parts = lax.axis_size("aa"), lax.axis_size("ba")
    fits = r % 16 == 0 and n == 8 and depth % AD == 0 and stretches == 2 and heads == 2
    fits = fits and 2 * rows == WINDOW and rows % (16 * parts) == 0
    return (local_blocks if fits else local)(*args)


def solution(mesh):
    token = P(None, "aa", "ba")
    hidden = P("aa", None, "ba", None)
    return jax.shard_map(
        pick,
        mesh=mesh,
        in_specs=(token,) * 7 + (hidden, P()),
        out_specs=(P(None, ("aa", "ba"), None), hidden, hidden),
        check_vma=False,
    )
```

```python
import functools
import math

import jax
import jax.numpy as jnp
from jax import lax
from jax.experimental import pallas as pl
from jax.experimental.pallas import tpu as pltpu
from jax.sharding import PartitionSpec as P

AD = 128
WINDOW = 512


BETA = 0.9
EPS = 1e-06


def shift(x, axis, by):
    length = lax.axis_size(axis)
    return lax.ppermute(x, axis, [(i, (i + by) % length) for i in range(length)])


def activation(x):
    sig = jax.nn.sigmoid(x)
    return (x * sig, sig * (1.0 + x * (1.0 - sig)))


def project(x, w):
    return jnp.einsum("nhd,hfd->nhf", x, w, preferred_element_type=jnp.float32)


def forward(w, query):
    rows, heads = query.shape[0], w.shape[1]
    q = query.reshape(rows, heads, -1)
    act_q, _ = activation(project(q, w[0]))
    hidden_q = (act_q * project(q, w[1])).astype(jnp.bfloat16)
    return jnp.einsum("nhf,hfd->nhd", hidden_q, w[2], preferred_element_type=jnp.float32).reshape(
        rows, -1
    )


def partial_grads(w, key, value, rate):
    rows, heads = key.shape[0], w.shape[1]
    k = key.reshape(rows, heads, -1)
    v = value.reshape(rows, heads, -1)
    gate_in = project(k, w[0])
    up_in = project(k, w[1])
    back_in = project(v, w[2])
    act, slope = activation(gate_in)
    gate_x = (rate[..., 0:1] * (-back_in * up_in * slope)).astype(jnp.bfloat16)
    up_x = (rate[..., 1:2] * (-back_in * act)).astype(jnp.bfloat16)
    down_x = (rate[..., 2:3] * -(act * up_in)).astype(jnp.bfloat16)

    def part(left, right):
        return jnp.einsum("nhf,nhd->hfd", left, right, preferred_element_type=jnp.float32)

    return jnp.stack([part(gate_x, k), part(up_x, k), part(down_x, v)]).astype(jnp.bfloat16)


def attend_kernel(rows, groups, q_ref, *refs):
    out_ref = refs[-1]
    stretch = pl.program_id(0)
    base = stretch * (rows * groups) + lax.axis_index("aa") * rows
    q = q_ref[0]
    scores = []
    blocks = (len(refs) - 1) // 2
    row = lax.broadcasted_iota(jnp.int32, (rows, rows), 0)
    col = lax.broadcasted_iota(jnp.int32, (rows, rows), 1)
    for back in range(blocks):
        s = lax.dot_general(
            q, refs[back][0], (((1,), (1,)), ((), ())), preferred_element_type=jnp.float32
        ) / math.sqrt(AD)
        gap = row - col + back * rows
        ok = (gap >= 0) & (gap < WINDOW) & (col >= back * rows - base)
        scores.append(jnp.where(ok, s, -1e30))
    top = functools.reduce(jnp.maximum, [jnp.max(s, -1, keepdims=True) for s in scores])
    total = 0.0
    acc = 0.0
    for back in range(blocks):
        p = jnp.exp(scores[back] - top)
        total = total + jnp.sum(p, -1, keepdims=True)
        acc = acc + jnp.dot(
            p.astype(jnp.bfloat16), refs[blocks + back][0], preferred_element_type=jnp.float32
        )
    out_ref[0] = acc / total


def attend(q, keys, values):
    stretches, rows, width = q.shape
    groups = lax.axis_size("aa")
    own = pl.BlockSpec((1, rows, AD), lambda s, h: (s, 0, h))
    index = lax.axis_index("aa")

    def moved(x, back):
        if not back:
            return x
        return jnp.where(index < back, jnp.concatenate([x[:1], x[:-1]], 0), x)

    keys = [moved(x, b) for b, x in enumerate(keys)]
    values = [moved(x, b) for b, x in enumerate(values)]
    return pl.pallas_call(
        functools.partial(attend_kernel, rows, groups),
        grid=(stretches, width // AD),
        in_specs=[own] * (1 + 2 * len(keys)),
        out_specs=own,
        out_shape=jax.ShapeDtypeStruct(q.shape, jnp.float32),
        cost_estimate=pl.CostEstimate(
            flops=4 * stretches * rows * rows * len(keys) * width,
            bytes_accessed=40 * q.size,
            transcendentals=stretches * rows * rows * len(keys) * width // AD,
        ),
        name="attend",
    )(q, *keys, *values)


def sum_kernel(n, x_ref, out_ref, land, send_sem, recv_sem):
    me = lax.axis_index("aa")
    barrier = pltpu.get_barrier_semaphore()
    for step in range(1, n):
        pl.semaphore_signal(
            barrier,
            inc=1,
            device_id={"aa": lax.rem(me + step, n)},
            device_id_type=pl.DeviceIdType.MESH,
        )
    pl.semaphore_wait(barrier, n - 1)
    copies = []
    for step in range(1, n):
        copy = pltpu.make_async_remote_copy(
            src_ref=x_ref,
            dst_ref=land.at[step],
            send_sem=send_sem.at[step],
            recv_sem=recv_sem.at[step],
            device_id={"aa": lax.rem(me + step, n)},
            device_id_type=pl.DeviceIdType.MESH,
        )
        copy.start()
        copies.append(copy)
    total = x_ref[...]
    for step in range(1, n):
        copies[step - 1].wait_recv()
        total = total + land[step]
    for copy in copies:
        copy.wait_send()
    out_ref[...] = total


def sum_over(x):
    n = lax.axis_size("aa")
    vmem = pl.BlockSpec(memory_space=pltpu.VMEM)
    return pl.pallas_call(
        functools.partial(sum_kernel, n),
        in_specs=[vmem],
        out_specs=vmem,
        out_shape=jax.ShapeDtypeStruct(x.shape, x.dtype),
        scratch_shapes=[
            pltpu.VMEM((n,) + x.shape, x.dtype),
            pltpu.SemaphoreType.DMA((n,)),
            pltpu.SemaphoreType.DMA((n,)),
        ],
        compiler_params=pltpu.CompilerParams(collective_id=1, has_side_effects=True),
        name="sum_over",
    )(x)


def tie(values, anchor):
    out = lax.optimization_barrier(tuple(values) + (anchor,))
    return out[:-1], out[-1]


def local(
    fast_query, fast_key, fast_value, rates, attn_query, attn_key, attn_value, fast_weights, gain
):
    stretches, rows, width = fast_query.shape
    local_rows = fast_weights.shape[0]
    heads = fast_weights.shape[2]
    rate = rates.reshape(stretches, rows, heads, 3)
    index = lax.axis_index("aa")
    groups = lax.axis_size("aa")
    first_row = index * local_rows

    shard = jnp.transpose(fast_weights, (1, 2, 0, 3))
    wb = lax.all_gather(shard.astype(jnp.bfloat16), "aa", axis=2, tiled=True)
    (attn_key, attn_value), wb = tie((attn_key, attn_value), wb)
    far = [shift(attn_key, "aa", 2), shift(attn_value, "aa", 2)]

    full = wb.astype(jnp.float32)
    target = jnp.sqrt(jnp.sum(full * full, 2, keepdims=True) + EPS)
    gp = partial_grads(wb, fast_key[0], fast_value[0], rate[0])
    grads = lax.psum(gp, "aa").astype(jnp.float32)

    (fq,), _ = tie((fast_query,), gp)
    out0 = forward(wb, fq[0])
    far, out0 = tie(far, out0)
    odd = index % 2 == 1
    swap = [(i, i ^ 1) for i in range(groups)]
    near = [
        lax.ppermute(jnp.where(odd, f, o), "aa", swap) for f, o in zip(far, (attn_key, attn_value))
    ]
    attention = attend(
        attn_query, [attn_key, near[0], far[0]], [attn_value, near[1], far[1]]
    )
    (attention,), grads = tie((attention,), grads)

    trial = full - grads
    updated = trial * (target / jnp.sqrt(jnp.sum(trial * trial, 2, keepdims=True) + EPS))
    ub = updated.astype(jnp.bfloat16)
    gp1 = partial_grads(ub, fast_key[1], fast_value[1], rate[1])
    grads1 = lax.psum_scatter(gp1, "aa", scatter_dimension=2, tiled=True).astype(jnp.float32)
    (fq1,), _ = tie((fast_query,), gp1)
    out1 = forward(ub, fq1[1])
    combined = (jnp.stack([out0, out1]) + attention).astype(jnp.bfloat16)

    moment = BETA * lax.dynamic_slice_in_dim(grads, first_row, local_rows, 2) + grads1
    own = lax.dynamic_slice_in_dim(updated, first_row, local_rows, 2)
    trial = own - moment
    squares = sum_over(jnp.sum(trial * trial, 2).reshape(-1, trial.shape[3]))
    squares = squares.reshape(trial.shape[:2] + (1, trial.shape[3]))
    weights = trial * (target / jnp.sqrt(squares + EPS))

    arrived = lax.all_to_all(combined, "ba", split_axis=1, concat_axis=2, tiled=True)
    values = arrived.astype(jnp.float32)
    scale = lax.rsqrt(jnp.mean(values * values, -1, keepdims=True) + EPS)
    mixed = (values * scale * gain).astype(jnp.bfloat16)
    back = (2, 0, 1, 3)
    return (mixed, jnp.transpose(weights, back), jnp.transpose(moment, back))


class Comm:
    def __init__(self, send, recv):
        self.send, self.recv, self.used = send, recv, 0

    def slots(self, count):
        first = self.used
        self.used += count
        return first

    def make(self, slot, src, dst, peer, lands=None):
        return pltpu.make_async_remote_copy(
            src_ref=src,
            dst_ref=dst,
            send_sem=self.send.at[slot],
            recv_sem=self.recv.at[slot if lands is None else lands],
            device_id=peer,
            device_id_type=pl.DeviceIdType.MESH,
        )


NT = (((1,), (1,)), ((), ()))
TN = (((0,), (0,)), ((), ()))
NN = (((1,), (0,)), ((), ()))


def block_kernel(
    n,
    parts,
    fq,
    fk,
    fv,
    rate,
    aq,
    ak,
    av,
    shard,
    gain,
    mixed,
    weights,
    moment,
    first,
    second,
    gp,
    pair,
    sums,
    landed,
    last_sums,
    last_landed,
    kb,
    vb,
    qb,
    xs,
    rate_rows,
    rate_far,
    aqb,
    akb,
    avb,
    far,
    near,
    relay,
    fast,
    back,
    comb,
    land,
    past,
    held_w,
    goal,
    goal_far,
    w_far,
    m_out,
    m_far,
    sq,
    loads,
    send,
    recv,
):
    me = lax.axis_index("aa")
    mine = lax.axis_index("ba")
    group, core = me // 2, lax.rem(me, 2)
    teams = n // 2
    heads, _, r, depth = shard.shape
    stretches, rows, width = fq.shape
    row_at, col_at = group // 2, lax.rem(group, 2)
    other = 1 - row_at
    beside = row_at * 2 + 1 - col_at
    above = other * 2 + col_at
    across = other * 2 + 1 - col_at
    partner = {"aa": group * 2 + 1 - core}
    to_x = {"aa": beside * 2 + core}
    to_y = {"aa": above * 2 + core}
    comm = Comm(send, recv)
    bf, f32 = jnp.bfloat16, jnp.float32
    tail = []

    def cols_of(h):
        return pl.ds(pl.multiple_of(h * depth, AD), depth)

    def slot_of(g):
        return core * teams + g

    def mm(a, b, dims):
        return lax.dot_general(a, b, dims, preferred_element_type=f32)

    def run(*args):
        copy = comm.make(comm.slots(1), *args)
        copy.start()
        tail.append(copy)
        return copy

    def drained(copy):
        copy.wait_send()
        tail[:] = [c for c in tail if c is not copy]

    barrier = pltpu.get_barrier_semaphore()
    for step in range(1, n):
        pl.semaphore_signal(
            barrier,
            inc=1,
            device_id={"aa": lax.rem(me + step, n)},
            device_id_type=pl.DeviceIdType.MESH,
        )
    for step in range(1, parts):
        pl.semaphore_signal(
            barrier,
            inc=1,
            device_id={"ba": lax.rem(mine + step, parts)},
            device_id_type=pl.DeviceIdType.MESH,
        )

    local = {}

    def load(name, src, dst):
        copy = pltpu.make_async_copy(src, dst, loads.at[len(local)])
        copy.start()
        local[name] = copy

    own_rows, far_rows = pl.ds(0, rows), pl.ds(rows, rows)
    tokens = {"k": (fk, kb), "v": (fv, vb), "q": (fq, qb)}
    for s in range(stretches):
        for name, (src, dst) in tokens.items():
            load((name, s), src.at[s, :, cols_of(row_at)], dst.at[s, own_rows])
    for name, src, dst in (("aq", aq, aqb), ("ak", ak, akb), ("av", av, avb)):
        load(name, src, dst)
    pl.semaphore_wait(barrier, n + parts - 2)

    sent = {}

    def send_tokens(name, s):
        src, dst = tokens[name]
        sent[name, s] = run(src.at[s, :, cols_of(other)], dst.at[s, far_rows], to_y)

    held = (ak, av)
    held_here = (akb, avb)
    lots = stretches * heads
    final = comm.slots(2 * lots)
    relays = comm.slots(lots)
    swaps = comm.slots(2 * lots)

    def part_of(p):
        return pl.ds(p * depth, depth)

    def halo_copy(t, s, p, direct):
        at, cols = s * heads + p, part_of(p)
        src = held[t].at[s, :, cols]
        if direct:
            return comm.make(final + t * lots + at, src, far.at[t, s, :, cols], to_x)
        peer = (to_x, to_y)[t]
        return comm.make(final + t * lots + at, src, relay.at[s, :, cols], peer, relays + at)

    def relay_copy(t, s, p):
        at, cols = s * heads + p, part_of(p)
        return comm.make(
            relays + at,
            relay.at[s, :, cols],
            far.at[t, s, :, cols],
            (to_y, to_x)[t],
            final + t * lots + at,
        )

    def sends_far(s):
        return (col_at == 1) & ((group < teams - 1) | (s < stretches - 1))

    def relays_far(s):
        return (s < stretches - 1) | (group == 0) | (group == teams - 1)

    def receives(s):
        return (s < stretches - 1) | (group > 0)

    def halo(s, p):
        for t in range(2):

            @pl.when(col_at == 0)
            def _():
                halo_copy(t, s, p, True).start()

            @pl.when(sends_far(s))
            def _():
                halo_copy(t, s, p, False).start()

    def halo_relay(s, p):
        for t in range(2):

            @pl.when((col_at == t) & relays_far(s))
            def _():
                halo_copy(0, s, p, False).wait_recv()
                relay_copy(t, s, p).start()

    def swap_copy(t, s, p, src):
        cols = part_of(p)
        return comm.make(
            swaps + t * lots + s * heads + p,
            src[t].at[s, :, cols],
            near.at[t, s, :, cols],
            partner,
        )

    def halo_swap(s, p):
        for t in range(2):

            @pl.when(core == 0)
            def _():
                swap_copy(t, s, p, held_here).start()

            @pl.when(receives(s))
            def _():
                halo_copy(t, s, p, True).wait_recv()

            @pl.when((core == 1) & receives(s))
            def _():
                swap_copy(t, s, p, (far.at[0], far.at[1])).start()

        for t in range(2):

            @pl.when((core == 1) | receives(s))
            def _():
                swap_copy(t, s, p, held_here).wait_recv()

            @pl.when((core == 0) | receives(s))
            def _():
                swap_copy(t, s, p, held_here).wait_send()

    def halo_sent(s, p):
        for t in range(2):

            @pl.when((col_at == 0) | sends_far(s))
            def _():
                halo_copy(t, s, p, True).wait_send()

        @pl.when(relays_far(s))
        def _():
            relay_copy(0, s, p).wait_send()

    def whole(ref, m):
        return ref[m].reshape(n * r, depth)

    def columns_of(ref):
        rate_rows[...] = jnp.zeros_like(rate_rows)
        for s in range(stretches):
            for m in range(3):
                rate_rows[s, pl.ds(m, 1), :] = ref[m, pl.ds(s, 1), :]
        return [jnp.transpose(rate_rows[s]) for s in range(stretches)]

    def hidden(ref, s, part, rates):
        at = far_rows if part else own_rows
        k, v = kb[s, at], vb[s, at]
        gate_in = mm(k, whole(ref, 0), NT)
        up_in = mm(k, whole(ref, 1), NT)
        back_in = mm(v, whole(ref, 2), NT)
        act, slope = activation(gate_in)
        xs[0, at] = (rates[:, 0:1] * (-back_in * up_in * slope)).astype(bf)
        xs[1, at] = (rates[:, 1:2] * (-back_in * act)).astype(bf)
        xs[2, at] = (rates[:, 2:3] * -(act * up_in)).astype(bf)

    def grads(phase):
        copies = []
        for m in range(3):
            other_side = vb[phase] if m == 2 else kb[phase]
            gp[m] = mm(xs[m], other_side, TN).astype(bf).reshape(n, r, depth)
            copies.append(
                run(gp.at[m, pl.ds((1 - core) * teams, teams)], pair.at[phase, m], partner)
            )
        return copies

    def both(phase, m, g):
        return gp[m, slot_of(g)].astype(f32) + pair[phase, m, g].astype(f32)

    def forward(ref, s, part):
        q = qb[s, far_rows if part else own_rows]
        act, _ = activation(mm(q, whole(ref, 0), NT))
        inner = (act * mm(q, whole(ref, 1), NT)).astype(bf)
        out = mm(inner, whole(ref, 2), NN).astype(bf)
        if not part:
            fast[s, :, cols_of(row_at)] = out
            return None
        back[s] = out
        return run(back.at[s], fast.at[s, :, cols_of(row_at)], to_y)

    def attention(s, p):
        base = s * (rows * n) + me * rows
        places = [s] + [jnp.where(me < b, max(s - 1, 0), s) for b in (1, 2)]
        row = lax.broadcasted_iota(jnp.int32, (rows, rows), 0)
        col = lax.broadcasted_iota(jnp.int32, (rows, rows), 1)
        oks = []
        for behind in range(3):
            gap = row - col + behind * rows
            oks.append((gap >= 0) & (gap < WINDOW) & (col >= behind * rows - base))

        @pl.loop(p * (depth // AD), (p + 1) * (depth // AD))
        def _(h):
            cols = pl.ds(pl.multiple_of(h * AD, AD), AD)
            keys = [akb[s, :, cols], near[0, places[1], :, cols], far[0, places[2], :, cols]]
            values = [avb[s, :, cols], near[1, places[1], :, cols], far[1, places[2], :, cols]]
            q = aqb[s, :, cols]
            scores = [
                jnp.where(ok, mm(q, k, NT) / math.sqrt(AD), -1e30) for ok, k in zip(oks, keys)
            ]
            top = functools.reduce(
                jnp.maximum, [jnp.max(x, -1, keepdims=True) for x in scores]
            )
            total, out = 0.0, 0.0
            for x, v in zip(scores, values):
                p = jnp.exp(x - top)
                total = total + jnp.sum(p, -1, keepdims=True)
                out = out + mm(p.astype(bf), v, NN)
            comb[s, :, cols] = (fast[s, :, cols].astype(f32) + out / total).astype(bf)

    def exchange(s, p):
        first_slot = comm.slots(parts)
        chunk = rows // parts
        copies = []
        for step in range(1, parts):
            z = lax.rem(mine + step, parts)
            take = pl.ds(pl.multiple_of(z * chunk, chunk), chunk)
            copy = comm.make(
                first_slot + step,
                comb.at[s, take, part_of(p)],
                land.at[s, step, :, part_of(p)],
                {"ba": z},
            )
            copy.start()
            copies.append(copy)
        return copies

    def finish(s, copies):
        chunk = rows // parts
        take = pl.ds(pl.multiple_of(mine * chunk, chunk), chunk)
        land[s, 0] = comb[s, take]
        for copy in copies:
            copy.wait()
        squares = 0.0
        for step in range(parts):
            x = land[s, step].astype(f32)
            squares = squares + jnp.sum(x * x, -1, keepdims=True)
        scale = lax.rsqrt(squares / (parts * width) + EPS)
        for step in range(parts):
            z = lax.rem(mine + parts - step, parts)
            cols = pl.ds(pl.multiple_of(z * width, 128), width)
            x = land[s, step].astype(f32)
            mixed[s, :, cols] = (x * scale * gain[:, cols]).astype(bf)

    def renorm(m):
        before, after = 0.0, 0.0
        for j in range(n):
            w = first[m, j].astype(f32)
            t = w - second[m, j].astype(f32)
            before = before + jnp.sum(w * w, 0, keepdims=True)
            after = after + jnp.sum(t * t, 0, keepdims=True)
        target = jnp.sqrt(before + EPS)
        goal[m] = target
        ratio = target / jnp.sqrt(after + EPS)
        for b, g in enumerate((group, above)):
            grad = second[m, slot_of(g)].astype(f32)
            past[b, m] = BETA * grad
            held_w[b, m] = (first[m, slot_of(g)].astype(f32) - grad) * ratio
        for j in range(n):
            w = first[m, j].astype(f32)
            t = w - second[m, j].astype(f32)
            second[m, j] = (t * ratio).astype(bf)

    here, near_y, near_x = slot_of(group), slot_of(above), slot_of(beside)
    corner = slot_of(across)
    up = run(shard.at[other], first.at[:, here], to_y)
    side = run(shard.at[row_at], first.at[:, here], to_x)
    twins = [run(shard.at[row_at], first.at[:, here], partner)]
    rate_copy = run(rate.at[pl.ds(3 * other, 3)], rate_far, to_y)
    first[:, here] = shard[row_at]
    rates = columns_of(rate.at[pl.ds(3 * row_at, 3)])
    up.wait_recv()
    onward = run(first.at[:, near_y], first.at[:, near_y], to_x)
    twins.append(run(first.at[:, near_y], first.at[:, near_y], partner))
    send_tokens("k", 0)
    send_tokens("v", 0)
    side.wait_recv()
    twins.append(run(first.at[:, near_x], first.at[:, near_x], partner))
    for p in range(heads):
        halo(0, p)
    onward.wait_recv()
    twins.append(run(first.at[:, corner], first.at[:, corner], partner))
    for copy in twins:
        copy.wait_recv()

    local["k", 0].wait()
    local["v", 0].wait()
    hidden(first, 0, 0, rates[0])
    rate_copy.wait_recv()
    far_rates = columns_of(rate_far)
    local["q", 0].wait()
    forward(first, 0, 0)
    sent["k", 0].wait_recv()
    sent["v", 0].wait_recv()
    send_tokens("q", 0)
    hidden(first, 0, 1, far_rates[0])
    pairs = grads(0)
    crossing = []
    for m in range(3):
        pairs[m].wait_recv()
        for g in range(teams):
            sums[m, g] = both(0, m, g).astype(bf)
        crossing.append(run(sums.at[m], landed.at[m], to_x))
    send_tokens("k", 1)
    send_tokens("v", 1)
    sent["q", 0].wait_recv()
    send_tokens("q", 1)
    arriving = forward(first, 0, 1)
    for p in range(heads):
        halo_relay(0, p)
    halo(1, 0)
    half = pl.ds(core * teams, teams)
    twins = []
    for m in range(3):
        crossing[m].wait_recv()
        second[m, half] = (sums[m].astype(f32) + landed[m].astype(f32)).astype(bf)
        twins.append(run(second.at[m, half], second.at[m, half], partner))
    halo(1, 1)
    for m in range(3):
        twins[m].wait_recv()
        drained(twins[m])
        drained(pairs[m])
        renorm(m)
    w_copy = run(second.at[:, near_y], w_far, to_y)
    goal_copy = run(goal, goal_far, to_y)
    for name in "kv":
        local[name, 1].wait()
        sent[name, 1].wait_recv()
    hidden(second, 1, 0, rates[1])
    hidden(second, 1, 1, far_rates[1])
    pairs = grads(1)
    crossing = []
    for m in range(3):
        pairs[m].wait_recv()
        for k in range(2):
            last_sums[m, k] = both(1, m, k * 2 + 1 - col_at).astype(bf)
        crossing.append(run(last_sums.at[m], last_landed.at[m], to_x))
    local["q", 1].wait()
    forward(second, 1, 0)
    for name in ("aq", "ak", "av"):
        local[name].wait()
    arriving.wait_recv()
    mixing0 = []
    for p in range(heads):
        halo_swap(0, p)
        attention(0, p)
        mixing0 += exchange(0, p)
    sent["q", 1].wait_recv()
    arriving = forward(second, 1, 1)
    for p in range(heads):
        halo_relay(1, p)
    finish(0, mixing0)
    arriving.wait_recv()
    mixing1 = []
    for p in range(heads):
        halo_swap(1, p)
        attention(1, p)
        mixing1 += exchange(1, p)
    m_copies = []
    for m in range(3):
        crossing[m].wait_recv()
        squares = 0.0
        for b, (g, k) in enumerate(((group, row_at), (above, other))):
            momentum = past[b, m] + both(1, m, g) + last_landed[m, k].astype(f32)
            trial = held_w[b, m] - momentum
            squares = squares + jnp.sum(trial * trial, 0, keepdims=True)
            if b:
                m_out[m] = momentum.astype(bf)
            else:
                moment[row_at, m] = momentum
                weights[row_at, m] = trial
        m_copies.append(run(m_out.at[m], m_far.at[m], to_y))
        sq[me, m] = squares
    first_slot = comm.slots(n)
    copies = []
    for step in range(1, n):
        copy = comm.make(
            first_slot + step, sq.at[me], sq.at[me], {"aa": lax.rem(me + step, n)}
        )
        copy.start()
        copies.append(copy)
    for copy in copies:
        copy.wait()
    w_copy.wait_recv()
    goal_copy.wait_recv()
    for m in range(3):
        m_copies[m].wait_recv()
        squares, squares_far = 0.0, 0.0
        for j in range(teams):
            squares = squares + sq[row_at * teams + j, m]
            squares_far = squares_far + sq[other * teams + j, m]
        weights[row_at, m] = weights[row_at, m] * (goal[m] / jnp.sqrt(squares + EPS))
        momentum = m_far[m].astype(f32)
        moment[other, m] = momentum
        weights[other, m] = (w_far[m].astype(f32) - momentum) * (
            goal_far[m] / jnp.sqrt(squares_far + EPS)
        )
    finish(1, mixing1)
    for copy in tail:
        copy.wait_send()
    for s in range(stretches):
        for p in range(heads):
            halo_sent(s, p)


def run_blocks(fq, fk, fv, rates, aq, ak, av, shard, gain):
    n, parts = lax.axis_size("aa"), lax.axis_size("ba")
    stretches, rows, width = fq.shape
    heads, _, r, depth = shard.shape
    teams = n // 2
    vmem = pl.BlockSpec(memory_space=pltpu.VMEM)
    hbm = pl.BlockSpec(memory_space=pl.ANY)
    piece = (r, depth)
    bf, f32 = jnp.bfloat16, jnp.float32
    slots = 5 * stretches * heads + 2 * heads * parts + n + 64
    token = pltpu.VMEM((stretches, 2 * rows, depth), bf)
    features = pltpu.VMEM((stretches, rows, width), bf)
    return pl.pallas_call(
        functools.partial(block_kernel, n, parts),
        in_specs=[hbm] * 3 + [vmem] + [hbm] * 3 + [vmem] * 2,
        out_specs=(vmem,) * 3,
        out_shape=(
            jax.ShapeDtypeStruct((stretches, rows // parts, width * parts), bf),
            jax.ShapeDtypeStruct((heads, 3) + piece, f32),
            jax.ShapeDtypeStruct((heads, 3) + piece, f32),
        ),
        scratch_shapes=[
            pltpu.VMEM((3, n) + piece, bf),
            pltpu.VMEM((3, n) + piece, bf),
            pltpu.VMEM((3, n) + piece, bf),
            pltpu.VMEM((2, 3, teams) + piece, bf),
            pltpu.VMEM((3, teams) + piece, bf),
            pltpu.VMEM((3, teams) + piece, bf),
            pltpu.VMEM((3, 2) + piece, bf),
            pltpu.VMEM((3, 2) + piece, bf),
            token,
            token,
            token,
            pltpu.VMEM((3, 2 * rows, depth), bf),
            pltpu.VMEM((stretches, 8, rows), f32),
            pltpu.VMEM((3, stretches, rows), f32),
            features,
            features,
            features,
            pltpu.VMEM((2, stretches, rows, width), bf),
            pltpu.VMEM((2, stretches, rows, width), bf),
            features,
            features,
            pltpu.VMEM((stretches, rows, depth), bf),
            features,
            pltpu.VMEM((stretches, parts, rows // parts, width), bf),
            pltpu.VMEM((2, 3) + piece, f32),
            pltpu.VMEM((2, 3) + piece, f32),
            pltpu.VMEM((3, 1, depth), f32),
            pltpu.VMEM((3, 1, depth), f32),
            pltpu.VMEM((3,) + piece, bf),
            pltpu.VMEM((3,) + piece, bf),
            pltpu.VMEM((3,) + piece, bf),
            pltpu.VMEM((n, 3, 1, depth), f32),
            pltpu.SemaphoreType.DMA((3 * stretches + 3,)),
            pltpu.SemaphoreType.DMA((slots,)),
            pltpu.SemaphoreType.DMA((slots,)),
        ],
        compiler_params=pltpu.CompilerParams(
            collective_id=2, has_side_effects=True, vmem_limit_bytes=67043328
        ),
        name="blocks",
    )(fq, fk, fv, rates, aq, ak, av, shard, gain)


def local_blocks(fq, fk, fv, rates, aq, ak, av, fast_weights, gain):
    shard = jnp.transpose(fast_weights.astype(jnp.bfloat16), (2, 1, 0, 3))
    rate = jnp.transpose(rates, (2, 0, 1))
    mixed, weights, moment = run_blocks(fq, fk, fv, rate, aq, ak, av, shard, gain[None])
    back = (2, 1, 0, 3)
    return (mixed, jnp.transpose(weights, back), jnp.transpose(moment, back))


def pick(*args):
    stretches, rows, _ = args[0].shape
    r, _, heads, depth = args[7].shape
    n, parts = lax.axis_size("aa"), lax.axis_size("ba")
    fits = r % 16 == 0 and n == 8 and depth % AD == 0 and stretches == 2 and heads == 2
    fits = fits and 2 * rows == WINDOW and rows % (16 * parts) == 0
    return (local_blocks if fits else local)(*args)


def solution(mesh):
    token = P(None, "aa", "ba")
    hidden = P("aa", None, "ba", None)
    return jax.shard_map(
        pick,
        mesh=mesh,
        in_specs=(token,) * 7 + (hidden, P()),
        out_specs=(P(None, ("aa", "ba"), None), hidden, hidden),
        check_vma=False,
    )
```

```python
import functools
import math

import jax
import jax.numpy as jnp
from jax import lax
from jax.experimental import pallas as pl
from jax.experimental.pallas import tpu as pltpu
from jax.sharding import PartitionSpec as P

AD = 128
WINDOW = 512


BETA = 0.9
EPS = 1e-06


def shift(x, axis, by):
    length = lax.axis_size(axis)
    return lax.ppermute(x, axis, [(i, (i + by) % length) for i in range(length)])


def activation(x):
    sig = jax.nn.sigmoid(x)
    return (x * sig, sig * (1.0 + x * (1.0 - sig)))


def project(x, w):
    return jnp.einsum("nhd,hfd->nhf", x, w, preferred_element_type=jnp.float32)


def forward(w, query):
    rows, heads = query.shape[0], w.shape[1]
    q = query.reshape(rows, heads, -1)
    act_q, _ = activation(project(q, w[0]))
    hidden_q = (act_q * project(q, w[1])).astype(jnp.bfloat16)
    return jnp.einsum("nhf,hfd->nhd", hidden_q, w[2], preferred_element_type=jnp.float32).reshape(
        rows, -1
    )


def partial_grads(w, key, value, rate):
    rows, heads = key.shape[0], w.shape[1]
    k = key.reshape(rows, heads, -1)
    v = value.reshape(rows, heads, -1)
    gate_in = project(k, w[0])
    up_in = project(k, w[1])
    back_in = project(v, w[2])
    act, slope = activation(gate_in)
    gate_x = (rate[..., 0:1] * (-back_in * up_in * slope)).astype(jnp.bfloat16)
    up_x = (rate[..., 1:2] * (-back_in * act)).astype(jnp.bfloat16)
    down_x = (rate[..., 2:3] * -(act * up_in)).astype(jnp.bfloat16)

    def part(left, right):
        return jnp.einsum("nhf,nhd->hfd", left, right, preferred_element_type=jnp.float32)

    return jnp.stack([part(gate_x, k), part(up_x, k), part(down_x, v)]).astype(jnp.bfloat16)


def attend_kernel(rows, groups, q_ref, *refs):
    out_ref = refs[-1]
    stretch = pl.program_id(0)
    base = stretch * (rows * groups) + lax.axis_index("aa") * rows
    q = q_ref[0]
    scores = []
    blocks = (len(refs) - 1) // 2
    row = lax.broadcasted_iota(jnp.int32, (rows, rows), 0)
    col = lax.broadcasted_iota(jnp.int32, (rows, rows), 1)
    for back in range(blocks):
        s = lax.dot_general(
            q, refs[back][0], (((1,), (1,)), ((), ())), preferred_element_type=jnp.float32
        ) / math.sqrt(AD)
        gap = row - col + back * rows
        ok = (gap >= 0) & (gap < WINDOW) & (col >= back * rows - base)
        scores.append(jnp.where(ok, s, -1e30))
    top = functools.reduce(jnp.maximum, [jnp.max(s, -1, keepdims=True) for s in scores])
    total = 0.0
    acc = 0.0
    for back in range(blocks):
        p = jnp.exp(scores[back] - top)
        total = total + jnp.sum(p, -1, keepdims=True)
        acc = acc + jnp.dot(
            p.astype(jnp.bfloat16), refs[blocks + back][0], preferred_element_type=jnp.float32
        )
    out_ref[0] = acc / total


def attend(q, keys, values):
    stretches, rows, width = q.shape
    groups = lax.axis_size("aa")
    own = pl.BlockSpec((1, rows, AD), lambda s, h: (s, 0, h))
    index = lax.axis_index("aa")

    def moved(x, back):
        if not back:
            return x
        return jnp.where(index < back, jnp.concatenate([x[:1], x[:-1]], 0), x)

    keys = [moved(x, b) for b, x in enumerate(keys)]
    values = [moved(x, b) for b, x in enumerate(values)]
    return pl.pallas_call(
        functools.partial(attend_kernel, rows, groups),
        grid=(stretches, width // AD),
        in_specs=[own] * (1 + 2 * len(keys)),
        out_specs=own,
        out_shape=jax.ShapeDtypeStruct(q.shape, jnp.float32),
        cost_estimate=pl.CostEstimate(
            flops=4 * stretches * rows * rows * len(keys) * width,
            bytes_accessed=40 * q.size,
            transcendentals=stretches * rows * rows * len(keys) * width // AD,
        ),
        name="attend",
    )(q, *keys, *values)


def sum_kernel(n, x_ref, out_ref, land, send_sem, recv_sem):
    me = lax.axis_index("aa")
    barrier = pltpu.get_barrier_semaphore()
    for step in range(1, n):
        pl.semaphore_signal(
            barrier,
            inc=1,
            device_id={"aa": lax.rem(me + step, n)},
            device_id_type=pl.DeviceIdType.MESH,
        )
    pl.semaphore_wait(barrier, n - 1)
    copies = []
    for step in range(1, n):
        copy = pltpu.make_async_remote_copy(
            src_ref=x_ref,
            dst_ref=land.at[step],
            send_sem=send_sem.at[step],
            recv_sem=recv_sem.at[step],
            device_id={"aa": lax.rem(me + step, n)},
            device_id_type=pl.DeviceIdType.MESH,
        )
        copy.start()
        copies.append(copy)
    total = x_ref[...]
    for step in range(1, n):
        copies[step - 1].wait_recv()
        total = total + land[step]
    for copy in copies:
        copy.wait_send()
    out_ref[...] = total


def sum_over(x):
    n = lax.axis_size("aa")
    vmem = pl.BlockSpec(memory_space=pltpu.VMEM)
    return pl.pallas_call(
        functools.partial(sum_kernel, n),
        in_specs=[vmem],
        out_specs=vmem,
        out_shape=jax.ShapeDtypeStruct(x.shape, x.dtype),
        scratch_shapes=[
            pltpu.VMEM((n,) + x.shape, x.dtype),
            pltpu.SemaphoreType.DMA((n,)),
            pltpu.SemaphoreType.DMA((n,)),
        ],
        compiler_params=pltpu.CompilerParams(collective_id=1, has_side_effects=True),
        name="sum_over",
    )(x)


def tie(values, anchor):
    out = lax.optimization_barrier(tuple(values) + (anchor,))
    return out[:-1], out[-1]


def local(
    fast_query, fast_key, fast_value, rates, attn_query, attn_key, attn_value, fast_weights, gain
):
    stretches, rows, width = fast_query.shape
    local_rows = fast_weights.shape[0]
    heads = fast_weights.shape[2]
    rate = rates.reshape(stretches, rows, heads, 3)
    index = lax.axis_index("aa")
    groups = lax.axis_size("aa")
    first_row = index * local_rows

    shard = jnp.transpose(fast_weights, (1, 2, 0, 3))
    wb = lax.all_gather(shard.astype(jnp.bfloat16), "aa", axis=2, tiled=True)
    (attn_key, attn_value), wb = tie((attn_key, attn_value), wb)
    far = [shift(attn_key, "aa", 2), shift(attn_value, "aa", 2)]

    full = wb.astype(jnp.float32)
    target = jnp.sqrt(jnp.sum(full * full, 2, keepdims=True) + EPS)
    gp = partial_grads(wb, fast_key[0], fast_value[0], rate[0])
    grads = lax.psum(gp, "aa").astype(jnp.float32)

    (fq,), _ = tie((fast_query,), gp)
    out0 = forward(wb, fq[0])
    far, out0 = tie(far, out0)
    odd = index % 2 == 1
    swap = [(i, i ^ 1) for i in range(groups)]
    near = [
        lax.ppermute(jnp.where(odd, f, o), "aa", swap) for f, o in zip(far, (attn_key, attn_value))
    ]
    attention = attend(
        attn_query, [attn_key, near[0], far[0]], [attn_value, near[1], far[1]]
    )
    (attention,), grads = tie((attention,), grads)

    trial = full - grads
    updated = trial * (target / jnp.sqrt(jnp.sum(trial * trial, 2, keepdims=True) + EPS))
    ub = updated.astype(jnp.bfloat16)
    gp1 = partial_grads(ub, fast_key[1], fast_value[1], rate[1])
    grads1 = lax.psum_scatter(gp1, "aa", scatter_dimension=2, tiled=True).astype(jnp.float32)
    (fq1,), _ = tie((fast_query,), gp1)
    out1 = forward(ub, fq1[1])
    combined = (jnp.stack([out0, out1]) + attention).astype(jnp.bfloat16)

    moment = BETA * lax.dynamic_slice_in_dim(grads, first_row, local_rows, 2) + grads1
    own = lax.dynamic_slice_in_dim(updated, first_row, local_rows, 2)
    trial = own - moment
    squares = sum_over(jnp.sum(trial * trial, 2).reshape(-1, trial.shape[3]))
    squares = squares.reshape(trial.shape[:2] + (1, trial.shape[3]))
    weights = trial * (target / jnp.sqrt(squares + EPS))

    arrived = lax.all_to_all(combined, "ba", split_axis=1, concat_axis=2, tiled=True)
    values = arrived.astype(jnp.float32)
    scale = lax.rsqrt(jnp.mean(values * values, -1, keepdims=True) + EPS)
    mixed = (values * scale * gain).astype(jnp.bfloat16)
    back = (2, 0, 1, 3)
    return (mixed, jnp.transpose(weights, back), jnp.transpose(moment, back))


class Comm:
    def __init__(self, send, recv):
        self.send, self.recv, self.used = send, recv, 0

    def slots(self, count):
        first = self.used
        self.used += count
        return first

    def make(self, slot, src, dst, peer, lands=None):
        return pltpu.make_async_remote_copy(
            src_ref=src,
            dst_ref=dst,
            send_sem=self.send.at[slot],
            recv_sem=self.recv.at[slot if lands is None else lands],
            device_id=peer,
            device_id_type=pl.DeviceIdType.MESH,
        )


NT = (((1,), (1,)), ((), ()))
TN = (((0,), (0,)), ((), ()))
NN = (((1,), (0,)), ((), ()))


def block_kernel(
    n,
    parts,
    fq,
    fk,
    fv,
    rate,
    aq,
    ak,
    av,
    shard,
    gain,
    mixed,
    weights,
    moment,
    first,
    second,
    gp,
    pair,
    sums,
    landed,
    last_sums,
    last_landed,
    kb,
    vb,
    qb,
    xs,
    rate_rows,
    rate_far,
    aqb,
    akb,
    avb,
    far,
    near,
    relay,
    fast,
    back,
    comb,
    land,
    past,
    held_w,
    goal,
    goal_far,
    w_far,
    m_out,
    m_far,
    sq,
    loads,
    send,
    recv,
):
    me = lax.axis_index("aa")
    mine = lax.axis_index("ba")
    group, core = me // 2, lax.rem(me, 2)
    teams = n // 2
    heads, _, r, depth = shard.shape
    stretches, rows, width = fq.shape
    row_at, col_at = group // 2, lax.rem(group, 2)
    other = 1 - row_at
    beside = row_at * 2 + 1 - col_at
    above = other * 2 + col_at
    across = other * 2 + 1 - col_at
    partner = {"aa": group * 2 + 1 - core}
    to_x = {"aa": beside * 2 + core}
    to_y = {"aa": above * 2 + core}
    comm = Comm(send, recv)
    bf, f32 = jnp.bfloat16, jnp.float32
    tail = []

    def cols_of(h):
        return pl.ds(pl.multiple_of(h * depth, AD), depth)

    def slot_of(g):
        return core * teams + g

    def mm(a, b, dims):
        return lax.dot_general(a, b, dims, preferred_element_type=f32)

    def run(*args):
        copy = comm.make(comm.slots(1), *args)
        copy.start()
        tail.append(copy)
        return copy

    def drained(copy):
        copy.wait_send()
        tail[:] = [c for c in tail if c is not copy]

    barrier = pltpu.get_barrier_semaphore()
    for step in range(1, n):
        pl.semaphore_signal(
            barrier,
            inc=1,
            device_id={"aa": lax.rem(me + step, n)},
            device_id_type=pl.DeviceIdType.MESH,
        )
    for step in range(1, parts):
        pl.semaphore_signal(
            barrier,
            inc=1,
            device_id={"ba": lax.rem(mine + step, parts)},
            device_id_type=pl.DeviceIdType.MESH,
        )

    local = {}

    def load(name, src, dst):
        copy = pltpu.make_async_copy(src, dst, loads.at[len(local)])
        copy.start()
        local[name] = copy

    own_rows, far_rows = pl.ds(0, rows), pl.ds(rows, rows)
    tokens = {"k": (fk, kb), "v": (fv, vb), "q": (fq, qb)}
    for s in range(stretches):
        for name, (src, dst) in tokens.items():
            load((name, s), src.at[s, :, cols_of(row_at)], dst.at[s, own_rows])
    for name, src, dst in (("aq", aq, aqb), ("ak", ak, akb), ("av", av, avb)):
        load(name, src, dst)
    pl.semaphore_wait(barrier, n + parts - 2)

    sent = {}

    def send_tokens(name, s):
        src, dst = tokens[name]
        sent[name, s] = run(src.at[s, :, cols_of(other)], dst.at[s, far_rows], to_y)

    held = (ak, av)
    held_here = (akb, avb)
    lots = stretches * heads
    final = comm.slots(2 * lots)
    relays = comm.slots(lots)
    swaps = comm.slots(2 * lots)

    def part_of(p):
        return pl.ds(p * depth, depth)

    def halo_copy(t, s, p, direct):
        at, cols = s * heads + p, part_of(p)
        src = held[t].at[s, :, cols]
        if direct:
            return comm.make(final + t * lots + at, src, far.at[t, s, :, cols], to_x)
        peer = (to_x, to_y)[t]
        return comm.make(final + t * lots + at, src, relay.at[s, :, cols], peer, relays + at)

    def relay_copy(t, s, p):
        at, cols = s * heads + p, part_of(p)
        return comm.make(
            relays + at,
            relay.at[s, :, cols],
            far.at[t, s, :, cols],
            (to_y, to_x)[t],
            final + t * lots + at,
        )

    def sends_far(s):
        return (col_at == 1) & ((group < teams - 1) | (s < stretches - 1))

    def relays_far(s):
        return (s < stretches - 1) | (group == 0) | (group == teams - 1)

    def receives(s):
        return (s < stretches - 1) | (group > 0)

    def halo(s, p):
        for t in range(2):

            @pl.when(col_at == 0)
            def _():
                halo_copy(t, s, p, True).start()

            @pl.when(sends_far(s))
            def _():
                halo_copy(t, s, p, False).start()

    def halo_relay(s, p):
        for t in range(2):

            @pl.when((col_at == t) & relays_far(s))
            def _():
                halo_copy(0, s, p, False).wait_recv()
                relay_copy(t, s, p).start()

    def swap_copy(t, s, p, src):
        cols = part_of(p)
        return comm.make(
            swaps + t * lots + s * heads + p,
            src[t].at[s, :, cols],
            near.at[t, s, :, cols],
            partner,
        )

    def halo_swap(s, p):
        for t in range(2):

            @pl.when(core == 0)
            def _():
                swap_copy(t, s, p, held_here).start()

            @pl.when(receives(s))
            def _():
                halo_copy(t, s, p, True).wait_recv()

            @pl.when((core == 1) & receives(s))
            def _():
                swap_copy(t, s, p, (far.at[0], far.at[1])).start()

        for t in range(2):

            @pl.when((core == 1) | receives(s))
            def _():
                swap_copy(t, s, p, held_here).wait_recv()

            @pl.when((core == 0) | receives(s))
            def _():
                swap_copy(t, s, p, held_here).wait_send()

    def halo_sent(s, p):
        for t in range(2):

            @pl.when((col_at == 0) | sends_far(s))
            def _():
                halo_copy(t, s, p, True).wait_send()

        @pl.when(relays_far(s))
        def _():
            relay_copy(0, s, p).wait_send()

    def whole(ref, m):
        return ref[m].reshape(n * r, depth)

    def columns_of(ref):
        rate_rows[...] = jnp.zeros_like(rate_rows)
        for s in range(stretches):
            for m in range(3):
                rate_rows[s, pl.ds(m, 1), :] = ref[m, pl.ds(s, 1), :]
        return [jnp.transpose(rate_rows[s]) for s in range(stretches)]

    def hidden(ref, s, part, rates):
        at = far_rows if part else own_rows
        k, v = kb[s, at], vb[s, at]
        gate_in = mm(k, whole(ref, 0), NT)
        up_in = mm(k, whole(ref, 1), NT)
        back_in = mm(v, whole(ref, 2), NT)
        act, slope = activation(gate_in)
        xs[0, at] = (rates[:, 0:1] * (-back_in * up_in * slope)).astype(bf)
        xs[1, at] = (rates[:, 1:2] * (-back_in * act)).astype(bf)
        xs[2, at] = (rates[:, 2:3] * -(act * up_in)).astype(bf)

    def grads(phase):
        copies = []
        for m in range(3):
            other_side = vb[phase] if m == 2 else kb[phase]
            gp[m] = mm(xs[m], other_side, TN).astype(bf).reshape(n, r, depth)
            copies.append(
                run(gp.at[m, pl.ds((1 - core) * teams, teams)], pair.at[phase, m], partner)
            )
        return copies

    def both(phase, m, g):
        return gp[m, slot_of(g)].astype(f32) + pair[phase, m, g].astype(f32)

    def forward(ref, s, part):
        q = qb[s, far_rows if part else own_rows]
        act, _ = activation(mm(q, whole(ref, 0), NT))
        inner = (act * mm(q, whole(ref, 1), NT)).astype(bf)
        out = mm(inner, whole(ref, 2), NN).astype(bf)
        if not part:
            fast[s, :, cols_of(row_at)] = out
            return None
        back[s] = out
        return run(back.at[s], fast.at[s, :, cols_of(row_at)], to_y)

    def attention(s, p):
        base = s * (rows * n) + me * rows
        places = [s] + [jnp.where(me < b, max(s - 1, 0), s) for b in (1, 2)]
        row = lax.broadcasted_iota(jnp.int32, (rows, rows), 0)
        col = lax.broadcasted_iota(jnp.int32, (rows, rows), 1)
        oks = []
        for behind in range(3):
            gap = row - col + behind * rows
            oks.append((gap >= 0) & (gap < WINDOW) & (col >= behind * rows - base))

        @pl.loop(p * (depth // AD), (p + 1) * (depth // AD))
        def _(h):
            cols = pl.ds(pl.multiple_of(h * AD, AD), AD)
            keys = [akb[s, :, cols], near[0, places[1], :, cols], far[0, places[2], :, cols]]
            values = [avb[s, :, cols], near[1, places[1], :, cols], far[1, places[2], :, cols]]
            q = aqb[s, :, cols]
            scores = [
                jnp.where(ok, mm(q, k, NT) / math.sqrt(AD), -1e30) for ok, k in zip(oks, keys)
            ]
            top = functools.reduce(
                jnp.maximum, [jnp.max(x, -1, keepdims=True) for x in scores]
            )
            total, out = 0.0, 0.0
            for x, v in zip(scores, values):
                p = jnp.exp(x - top)
                total = total + jnp.sum(p, -1, keepdims=True)
                out = out + mm(p.astype(bf), v, NN)
            comb[s, :, cols] = (fast[s, :, cols].astype(f32) + out / total).astype(bf)

    def exchange(s, p):
        first_slot = comm.slots(parts)
        chunk = rows // parts
        copies = []
        for step in range(1, parts):
            z = lax.rem(mine + step, parts)
            take = pl.ds(pl.multiple_of(z * chunk, chunk), chunk)
            copy = comm.make(
                first_slot + step,
                comb.at[s, take, part_of(p)],
                land.at[s, step, :, part_of(p)],
                {"ba": z},
            )
            copy.start()
            copies.append(copy)
        return copies

    def finish(s, copies):
        chunk = rows // parts
        take = pl.ds(pl.multiple_of(mine * chunk, chunk), chunk)
        land[s, 0] = comb[s, take]
        for copy in copies:
            copy.wait()
        squares = 0.0
        for step in range(parts):
            x = land[s, step].astype(f32)
            squares = squares + jnp.sum(x * x, -1, keepdims=True)
        scale = lax.rsqrt(squares / (parts * width) + EPS)
        for step in range(parts):
            z = lax.rem(mine + parts - step, parts)
            cols = pl.ds(pl.multiple_of(z * width, 128), width)
            x = land[s, step].astype(f32)
            mixed[s, :, cols] = (x * scale * gain[:, cols]).astype(bf)

    def renorm(m):
        before, after = 0.0, 0.0
        for j in range(n):
            w = first[m, j].astype(f32)
            t = w - second[m, j].astype(f32)
            before = before + jnp.sum(w * w, 0, keepdims=True)
            after = after + jnp.sum(t * t, 0, keepdims=True)
        target = jnp.sqrt(before + EPS)
        goal[m] = target
        ratio = target / jnp.sqrt(after + EPS)
        for b, g in enumerate((group, above)):
            grad = second[m, slot_of(g)].astype(f32)
            past[b, m] = BETA * grad
            held_w[b, m] = (first[m, slot_of(g)].astype(f32) - grad) * ratio
        for j in range(n):
            w = first[m, j].astype(f32)
            t = w - second[m, j].astype(f32)
            second[m, j] = (t * ratio).astype(bf)

    here, near_y, near_x = slot_of(group), slot_of(above), slot_of(beside)
    corner = slot_of(across)
    up = run(shard.at[other], first.at[:, here], to_y)
    side = run(shard.at[row_at], first.at[:, here], to_x)
    twins = [run(shard.at[row_at], first.at[:, here], partner)]
    rate_copy = run(rate.at[pl.ds(3 * other, 3)], rate_far, to_y)
    first[:, here] = shard[row_at]
    rates = columns_of(rate.at[pl.ds(3 * row_at, 3)])
    up.wait_recv()
    onward = run(first.at[:, near_y], first.at[:, near_y], to_x)
    twins.append(run(first.at[:, near_y], first.at[:, near_y], partner))
    send_tokens("k", 0)
    send_tokens("v", 0)
    side.wait_recv()
    twins.append(run(first.at[:, near_x], first.at[:, near_x], partner))
    for p in range(heads):
        halo(0, p)
    onward.wait_recv()
    twins.append(run(first.at[:, corner], first.at[:, corner], partner))
    for copy in twins:
        copy.wait_recv()

    local["k", 0].wait()
    local["v", 0].wait()
    hidden(first, 0, 0, rates[0])
    rate_copy.wait_recv()
    far_rates = columns_of(rate_far)
    local["q", 0].wait()
    forward(first, 0, 0)
    sent["k", 0].wait_recv()
    sent["v", 0].wait_recv()
    send_tokens("q", 0)
    hidden(first, 0, 1, far_rates[0])
    pairs = grads(0)
    crossing = []
    for m in range(3):
        pairs[m].wait_recv()
        for g in range(teams):
            sums[m, g] = both(0, m, g).astype(bf)
        crossing.append(run(sums.at[m], landed.at[m], to_x))
    send_tokens("k", 1)
    send_tokens("v", 1)
    sent["q", 0].wait_recv()
    send_tokens("q", 1)
    arriving = forward(first, 0, 1)
    for p in range(heads):
        halo_relay(0, p)
    halo(1, 0)
    half = pl.ds(core * teams, teams)
    twins = []
    for m in range(3):
        crossing[m].wait_recv()
        second[m, half] = (sums[m].astype(f32) + landed[m].astype(f32)).astype(bf)
        twins.append(run(second.at[m, half], second.at[m, half], partner))
    halo(1, 1)
    for m in range(3):
        twins[m].wait_recv()
        drained(twins[m])
        drained(pairs[m])
        renorm(m)
    w_copy = run(second.at[:, near_y], w_far, to_y)
    goal_copy = run(goal, goal_far, to_y)
    for name in "kv":
        local[name, 1].wait()
        sent[name, 1].wait_recv()
    hidden(second, 1, 0, rates[1])
    hidden(second, 1, 1, far_rates[1])
    pairs = grads(1)
    crossing = []
    for m in range(3):
        pairs[m].wait_recv()
        for k in range(2):
            last_sums[m, k] = both(1, m, k * 2 + 1 - col_at).astype(bf)
        crossing.append(run(last_sums.at[m], last_landed.at[m], to_x))
    local["q", 1].wait()
    forward(second, 1, 0)
    for name in ("aq", "ak", "av"):
        local[name].wait()
    arriving.wait_recv()
    mixing0 = []
    for p in range(heads):
        halo_swap(0, p)
        attention(0, p)
        mixing0 += exchange(0, p)
    sent["q", 1].wait_recv()
    arriving = forward(second, 1, 1)
    for p in range(heads):
        halo_relay(1, p)
    finish(0, mixing0)
    arriving.wait_recv()
    mixing1 = []
    for p in range(heads):
        halo_swap(1, p)
        attention(1, p)
        mixing1 += exchange(1, p)
    m_copies = []
    for m in range(3):
        crossing[m].wait_recv()
        squares = 0.0
        for b, (g, k) in enumerate(((group, row_at), (above, other))):
            momentum = past[b, m] + both(1, m, g) + last_landed[m, k].astype(f32)
            trial = held_w[b, m] - momentum
            squares = squares + jnp.sum(trial * trial, 0, keepdims=True)
            if b:
                m_out[m] = momentum.astype(bf)
            else:
                moment[row_at, m] = momentum
                weights[row_at, m] = trial
        m_copies.append(run(m_out.at[m], m_far.at[m], to_y))
        sq[me, m] = squares
    first_slot = comm.slots(n)
    copies = []
    for step in range(1, n):
        copy = comm.make(
            first_slot + step, sq.at[me], sq.at[me], {"aa": lax.rem(me + step, n)}
        )
        copy.start()
        copies.append(copy)
    for copy in copies:
        copy.wait()
    w_copy.wait_recv()
    goal_copy.wait_recv()
    for m in range(3):
        m_copies[m].wait_recv()
        squares, squares_far = 0.0, 0.0
        for j in range(teams):
            squares = squares + sq[row_at * teams + j, m]
            squares_far = squares_far + sq[other * teams + j, m]
        weights[row_at, m] = weights[row_at, m] * (goal[m] / jnp.sqrt(squares + EPS))
        momentum = m_far[m].astype(f32)
        moment[other, m] = momentum
        weights[other, m] = (w_far[m].astype(f32) - momentum) * (
            goal_far[m] / jnp.sqrt(squares_far + EPS)
        )
    finish(1, mixing1)
    for copy in tail:
        copy.wait_send()
    for s in range(stretches):
        for p in range(heads):
            halo_sent(s, p)


def run_blocks(fq, fk, fv, rates, aq, ak, av, shard, gain):
    n, parts = lax.axis_size("aa"), lax.axis_size("ba")
    stretches, rows, width = fq.shape
    heads, _, r, depth = shard.shape
    teams = n // 2
    vmem = pl.BlockSpec(memory_space=pltpu.VMEM)
    hbm = pl.BlockSpec(memory_space=pl.ANY)
    piece = (r, depth)
    bf, f32 = jnp.bfloat16, jnp.float32
    slots = 5 * stretches * heads + 2 * heads * parts + n + 64
    token = pltpu.VMEM((stretches, 2 * rows, depth), bf)
    features = pltpu.VMEM((stretches, rows, width), bf)
    return pl.pallas_call(
        functools.partial(block_kernel, n, parts),
        in_specs=[hbm] * 3 + [vmem] + [hbm] * 3 + [vmem] * 2,
        out_specs=(vmem,) * 3,
        out_shape=(
            jax.ShapeDtypeStruct((stretches, rows // parts, width * parts), bf),
            jax.ShapeDtypeStruct((heads, 3) + piece, f32),
            jax.ShapeDtypeStruct((heads, 3) + piece, f32),
        ),
        scratch_shapes=[
            pltpu.VMEM((3, n) + piece, bf),
            pltpu.VMEM((3, n) + piece, bf),
            pltpu.VMEM((3, n) + piece, bf),
            pltpu.VMEM((2, 3, teams) + piece, bf),
            pltpu.VMEM((3, teams) + piece, bf),
            pltpu.VMEM((3, teams) + piece, bf),
            pltpu.VMEM((3, 2) + piece, bf),
            pltpu.VMEM((3, 2) + piece, bf),
            token,
            token,
            token,
            pltpu.VMEM((3, 2 * rows, depth), bf),
            pltpu.VMEM((stretches, 8, rows), f32),
            pltpu.VMEM((3, stretches, rows), f32),
            features,
            features,
            features,
            pltpu.VMEM((2, stretches, rows, width), bf),
            pltpu.VMEM((2, stretches, rows, width), bf),
            features,
            features,
            pltpu.VMEM((stretches, rows, depth), bf),
            features,
            pltpu.VMEM((stretches, parts, rows // parts, width), bf),
            pltpu.VMEM((2, 3) + piece, f32),
            pltpu.VMEM((2, 3) + piece, f32),
            pltpu.VMEM((3, 1, depth), f32),
            pltpu.VMEM((3, 1, depth), f32),
            pltpu.VMEM((3,) + piece, bf),
            pltpu.VMEM((3,) + piece, bf),
            pltpu.VMEM((3,) + piece, bf),
            pltpu.VMEM((n, 3, 1, depth), f32),
            pltpu.SemaphoreType.DMA((3 * stretches + 3,)),
            pltpu.SemaphoreType.DMA((slots,)),
            pltpu.SemaphoreType.DMA((slots,)),
        ],
        compiler_params=pltpu.CompilerParams(
            collective_id=2, has_side_effects=True, vmem_limit_bytes=51 * 2**20
        ),
        name="blocks",
    )(fq, fk, fv, rates, aq, ak, av, shard, gain)


def local_blocks(fq, fk, fv, rates, aq, ak, av, fast_weights, gain):
    shard = jnp.transpose(fast_weights.astype(jnp.bfloat16), (2, 1, 0, 3))
    rate = jnp.transpose(rates, (2, 0, 1))
    mixed, weights, moment = run_blocks(fq, fk, fv, rate, aq, ak, av, shard, gain[None])
    back = (2, 1, 0, 3)
    return (mixed, jnp.transpose(weights, back), jnp.transpose(moment, back))


def pick(*args):
    stretches, rows, _ = args[0].shape
    r, _, heads, depth = args[7].shape
    n, parts = lax.axis_size("aa"), lax.axis_size("ba")
    fits = r % 16 == 0 and n == 8 and depth % AD == 0 and stretches == 2 and heads == 2
    fits = fits and 2 * rows == WINDOW and rows % (16 * parts) == 0
    return (local_blocks if fits else local)(*args)


def solution(mesh):
    token = P(None, "aa", "ba")
    hidden = P("aa", None, "ba", None)
    return jax.shard_map(
        pick,
        mesh=mesh,
        in_specs=(token,) * 7 + (hidden, P()),
        out_specs=(P(None, ("aa", "ba"), None), hidden, hidden),
        check_vma=False,
    )
```

```python
import functools
import math

import jax
import jax.numpy as jnp
from jax import lax
from jax.experimental import pallas as pl
from jax.experimental.pallas import tpu as pltpu
from jax.sharding import PartitionSpec as P

AD = 128
WINDOW = 512


BETA = 0.9
EPS = 1e-06


def shift(x, axis, by):
    length = lax.axis_size(axis)
    return lax.ppermute(x, axis, [(i, (i + by) % length) for i in range(length)])


def activation(x):
    sig = jax.nn.sigmoid(x)
    return (x * sig, sig * (1.0 + x * (1.0 - sig)))


def project(x, w):
    return jnp.einsum("nhd,hfd->nhf", x, w, preferred_element_type=jnp.float32)


def forward(w, query):
    rows, heads = query.shape[0], w.shape[1]
    q = query.reshape(rows, heads, -1)
    act_q, _ = activation(project(q, w[0]))
    hidden_q = (act_q * project(q, w[1])).astype(jnp.bfloat16)
    return jnp.einsum("nhf,hfd->nhd", hidden_q, w[2], preferred_element_type=jnp.float32).reshape(
        rows, -1
    )


def partial_grads(w, key, value, rate):
    rows, heads = key.shape[0], w.shape[1]
    k = key.reshape(rows, heads, -1)
    v = value.reshape(rows, heads, -1)
    gate_in = project(k, w[0])
    up_in = project(k, w[1])
    back_in = project(v, w[2])
    act, slope = activation(gate_in)
    gate_x = (rate[..., 0:1] * (-back_in * up_in * slope)).astype(jnp.bfloat16)
    up_x = (rate[..., 1:2] * (-back_in * act)).astype(jnp.bfloat16)
    down_x = (rate[..., 2:3] * -(act * up_in)).astype(jnp.bfloat16)

    def part(left, right):
        return jnp.einsum("nhf,nhd->hfd", left, right, preferred_element_type=jnp.float32)

    return jnp.stack([part(gate_x, k), part(up_x, k), part(down_x, v)]).astype(jnp.bfloat16)


def attend_kernel(rows, groups, q_ref, *refs):
    out_ref = refs[-1]
    stretch = pl.program_id(0)
    base = stretch * (rows * groups) + lax.axis_index("aa") * rows
    q = q_ref[0]
    scores = []
    blocks = (len(refs) - 1) // 2
    row = lax.broadcasted_iota(jnp.int32, (rows, rows), 0)
    col = lax.broadcasted_iota(jnp.int32, (rows, rows), 1)
    for back in range(blocks):
        s = lax.dot_general(
            q, refs[back][0], (((1,), (1,)), ((), ())), preferred_element_type=jnp.float32
        ) / math.sqrt(AD)
        gap = row - col + back * rows
        ok = (gap >= 0) & (gap < WINDOW) & (col >= back * rows - base)
        scores.append(jnp.where(ok, s, -1e30))
    top = functools.reduce(jnp.maximum, [jnp.max(s, -1, keepdims=True) for s in scores])
    total = 0.0
    acc = 0.0
    for back in range(blocks):
        p = jnp.exp(scores[back] - top)
        total = total + jnp.sum(p, -1, keepdims=True)
        acc = acc + jnp.dot(
            p.astype(jnp.bfloat16), refs[blocks + back][0], preferred_element_type=jnp.float32
        )
    out_ref[0] = acc / total


def attend(q, keys, values):
    stretches, rows, width = q.shape
    groups = lax.axis_size("aa")
    own = pl.BlockSpec((1, rows, AD), lambda s, h: (s, 0, h))
    index = lax.axis_index("aa")

    def moved(x, back):
        if not back:
            return x
        return jnp.where(index < back, jnp.concatenate([x[:1], x[:-1]], 0), x)

    keys = [moved(x, b) for b, x in enumerate(keys)]
    values = [moved(x, b) for b, x in enumerate(values)]
    return pl.pallas_call(
        functools.partial(attend_kernel, rows, groups),
        grid=(stretches, width // AD),
        in_specs=[own] * (1 + 2 * len(keys)),
        out_specs=own,
        out_shape=jax.ShapeDtypeStruct(q.shape, jnp.float32),
        cost_estimate=pl.CostEstimate(
            flops=4 * stretches * rows * rows * len(keys) * width,
            bytes_accessed=40 * q.size,
            transcendentals=stretches * rows * rows * len(keys) * width // AD,
        ),
        name="attend",
    )(q, *keys, *values)


def sum_kernel(n, x_ref, out_ref, land, send_sem, recv_sem):
    me = lax.axis_index("aa")
    barrier = pltpu.get_barrier_semaphore()
    for step in range(1, n):
        pl.semaphore_signal(
            barrier,
            inc=1,
            device_id={"aa": lax.rem(me + step, n)},
            device_id_type=pl.DeviceIdType.MESH,
        )
    pl.semaphore_wait(barrier, n - 1)
    copies = []
    for step in range(1, n):
        copy = pltpu.make_async_remote_copy(
            src_ref=x_ref,
            dst_ref=land.at[step],
            send_sem=send_sem.at[step],
            recv_sem=recv_sem.at[step],
            device_id={"aa": lax.rem(me + step, n)},
            device_id_type=pl.DeviceIdType.MESH,
        )
        copy.start()
        copies.append(copy)
    total = x_ref[...]
    for step in range(1, n):
        copies[step - 1].wait_recv()
        total = total + land[step]
    for copy in copies:
        copy.wait_send()
    out_ref[...] = total


def sum_over(x):
    n = lax.axis_size("aa")
    vmem = pl.BlockSpec(memory_space=pltpu.VMEM)
    return pl.pallas_call(
        functools.partial(sum_kernel, n),
        in_specs=[vmem],
        out_specs=vmem,
        out_shape=jax.ShapeDtypeStruct(x.shape, x.dtype),
        scratch_shapes=[
            pltpu.VMEM((n,) + x.shape, x.dtype),
            pltpu.SemaphoreType.DMA((n,)),
            pltpu.SemaphoreType.DMA((n,)),
        ],
        compiler_params=pltpu.CompilerParams(collective_id=1, has_side_effects=True),
        name="sum_over",
    )(x)


def tie(values, anchor):
    out = lax.optimization_barrier(tuple(values) + (anchor,))
    return out[:-1], out[-1]


def local(
    fast_query, fast_key, fast_value, rates, attn_query, attn_key, attn_value, fast_weights, gain
):
    stretches, rows, width = fast_query.shape
    local_rows = fast_weights.shape[0]
    heads = fast_weights.shape[2]
    rate = rates.reshape(stretches, rows, heads, 3)
    index = lax.axis_index("aa")
    groups = lax.axis_size("aa")
    first_row = index * local_rows

    shard = jnp.transpose(fast_weights, (1, 2, 0, 3))
    wb = lax.all_gather(shard.astype(jnp.bfloat16), "aa", axis=2, tiled=True)
    (attn_key, attn_value), wb = tie((attn_key, attn_value), wb)
    far = [shift(attn_key, "aa", 2), shift(attn_value, "aa", 2)]

    full = wb.astype(jnp.float32)
    target = jnp.sqrt(jnp.sum(full * full, 2, keepdims=True) + EPS)
    gp = partial_grads(wb, fast_key[0], fast_value[0], rate[0])
    grads = lax.psum(gp, "aa").astype(jnp.float32)

    (fq,), _ = tie((fast_query,), gp)
    out0 = forward(wb, fq[0])
    far, out0 = tie(far, out0)
    odd = index % 2 == 1
    swap = [(i, i ^ 1) for i in range(groups)]
    near = [
        lax.ppermute(jnp.where(odd, f, o), "aa", swap) for f, o in zip(far, (attn_key, attn_value))
    ]
    attention = attend(
        attn_query, [attn_key, near[0], far[0]], [attn_value, near[1], far[1]]
    )
    (attention,), grads = tie((attention,), grads)

    trial = full - grads
    updated = trial * (target / jnp.sqrt(jnp.sum(trial * trial, 2, keepdims=True) + EPS))
    ub = updated.astype(jnp.bfloat16)
    gp1 = partial_grads(ub, fast_key[1], fast_value[1], rate[1])
    grads1 = lax.psum_scatter(gp1, "aa", scatter_dimension=2, tiled=True).astype(jnp.float32)
    (fq1,), _ = tie((fast_query,), gp1)
    out1 = forward(ub, fq1[1])
    combined = (jnp.stack([out0, out1]) + attention).astype(jnp.bfloat16)

    moment = BETA * lax.dynamic_slice_in_dim(grads, first_row, local_rows, 2) + grads1
    own = lax.dynamic_slice_in_dim(updated, first_row, local_rows, 2)
    trial = own - moment
    squares = sum_over(jnp.sum(trial * trial, 2).reshape(-1, trial.shape[3]))
    squares = squares.reshape(trial.shape[:2] + (1, trial.shape[3]))
    weights = trial * (target / jnp.sqrt(squares + EPS))

    arrived = lax.all_to_all(combined, "ba", split_axis=1, concat_axis=2, tiled=True)
    values = arrived.astype(jnp.float32)
    scale = lax.rsqrt(jnp.mean(values * values, -1, keepdims=True) + EPS)
    mixed = (values * scale * gain).astype(jnp.bfloat16)
    back = (2, 0, 1, 3)
    return (mixed, jnp.transpose(weights, back), jnp.transpose(moment, back))


class Comm:
    def __init__(self, send, recv):
        self.send, self.recv, self.used = send, recv, 0

    def slots(self, count):
        first = self.used
        self.used += count
        return first

    def make(self, slot, src, dst, peer, lands=None):
        return pltpu.make_async_remote_copy(
            src_ref=src,
            dst_ref=dst,
            send_sem=self.send.at[slot],
            recv_sem=self.recv.at[slot if lands is None else lands],
            device_id=peer,
            device_id_type=pl.DeviceIdType.MESH,
        )


NT = (((1,), (1,)), ((), ()))
TN = (((0,), (0,)), ((), ()))
NN = (((1,), (0,)), ((), ()))


def block_kernel(
    n,
    parts,
    fq,
    fk,
    fv,
    rate,
    aq,
    ak,
    av,
    shard,
    gain,
    mixed,
    weights,
    moment,
    first,
    second,
    gp,
    pair,
    sums,
    landed,
    last_sums,
    last_landed,
    kb,
    vb,
    qb,
    xs,
    rate_rows,
    rate_far,
    aqb,
    akb,
    avb,
    far,
    near,
    relay,
    fast,
    back,
    comb,
    land,
    past,
    held_w,
    goal,
    goal_far,
    w_far,
    m_out,
    m_far,
    sq,
    loads,
    send,
    recv,
):
    me = lax.axis_index("aa")
    mine = lax.axis_index("ba")
    group, core = me // 2, lax.rem(me, 2)
    teams = n // 2
    heads, _, r, depth = shard.shape
    stretches, rows, width = fq.shape
    row_at, col_at = group // 2, lax.rem(group, 2)
    other = 1 - row_at
    beside = row_at * 2 + 1 - col_at
    above = other * 2 + col_at
    across = other * 2 + 1 - col_at
    partner = {"aa": group * 2 + 1 - core}
    to_x = {"aa": beside * 2 + core}
    to_y = {"aa": above * 2 + core}
    comm = Comm(send, recv)
    bf, f32 = jnp.bfloat16, jnp.float32
    tail = []

    def cols_of(h):
        return pl.ds(pl.multiple_of(h * depth, AD), depth)

    def slot_of(g):
        return core * teams + g

    def mm(a, b, dims):
        return lax.dot_general(a, b, dims, preferred_element_type=f32)

    def run(*args):
        copy = comm.make(comm.slots(1), *args)
        copy.start()
        tail.append(copy)
        return copy

    def drained(copy):
        copy.wait_send()
        tail[:] = [c for c in tail if c is not copy]

    barrier = pltpu.get_barrier_semaphore()
    for step in range(1, n):
        pl.semaphore_signal(
            barrier,
            inc=1,
            device_id={"aa": lax.rem(me + step, n)},
            device_id_type=pl.DeviceIdType.MESH,
        )
    for step in range(1, parts):
        pl.semaphore_signal(
            barrier,
            inc=1,
            device_id={"ba": lax.rem(mine + step, parts)},
            device_id_type=pl.DeviceIdType.MESH,
        )

    local = {}

    def load(name, src, dst):
        copy = pltpu.make_async_copy(src, dst, loads.at[len(local)])
        copy.start()
        local[name] = copy

    own_rows, far_rows = pl.ds(0, rows), pl.ds(rows, rows)
    tokens = {"k": (fk, kb), "v": (fv, vb), "q": (fq, qb)}
    for s in range(stretches):
        for name, (src, dst) in tokens.items():
            load((name, s), src.at[s, :, cols_of(row_at)], dst.at[s, own_rows])
    for name, src, dst in (("aq", aq, aqb), ("ak", ak, akb), ("av", av, avb)):
        load(name, src, dst)
    pl.semaphore_wait(barrier, n + parts - 2)

    sent = {}

    def send_tokens(name, s):
        src, dst = tokens[name]
        sent[name, s] = run(src.at[s, :, cols_of(other)], dst.at[s, far_rows], to_y)

    held = (ak, av)
    held_here = (akb, avb)
    lots = stretches * heads
    final = comm.slots(2 * lots)
    relays = comm.slots(lots)
    swaps = comm.slots(2 * lots)

    def part_of(p):
        return pl.ds(p * depth, depth)

    def halo_copy(t, s, p, direct):
        at, cols = s * heads + p, part_of(p)
        src = held[t].at[s, :, cols]
        if direct:
            return comm.make(final + t * lots + at, src, far.at[t, s, :, cols], to_x)
        peer = (to_x, to_y)[t]
        return comm.make(final + t * lots + at, src, relay.at[s, :, cols], peer, relays + at)

    def relay_copy(t, s, p):
        at, cols = s * heads + p, part_of(p)
        return comm.make(
            relays + at,
            relay.at[s, :, cols],
            far.at[t, s, :, cols],
            (to_y, to_x)[t],
            final + t * lots + at,
        )

    def sends_far(s):
        return (col_at == 1) & ((group < teams - 1) | (s < stretches - 1))

    def relays_far(s):
        return (s < stretches - 1) | (group == 0) | (group == teams - 1)

    def receives(s):
        return (s < stretches - 1) | (group > 0)

    def halo(s, p):
        for t in range(2):

            @pl.when(col_at == 0)
            def _():
                halo_copy(t, s, p, True).start()

            @pl.when(sends_far(s))
            def _():
                halo_copy(t, s, p, False).start()

    def halo_relay(s, p):
        for t in range(2):

            @pl.when((col_at == t) & relays_far(s))
            def _():
                halo_copy(0, s, p, False).wait_recv()
                relay_copy(t, s, p).start()

    def swap_copy(t, s, p, src):
        cols = part_of(p)
        return comm.make(
            swaps + t * lots + s * heads + p,
            src[t].at[s, :, cols],
            near.at[t, s, :, cols],
            partner,
        )

    def halo_swap(s, p):
        for t in range(2):

            @pl.when(core == 0)
            def _():
                swap_copy(t, s, p, held_here).start()

            @pl.when(receives(s))
            def _():
                halo_copy(t, s, p, True).wait_recv()

            @pl.when((core == 1) & receives(s))
            def _():
                swap_copy(t, s, p, (far.at[0], far.at[1])).start()

        for t in range(2):

            @pl.when((core == 1) | receives(s))
            def _():
                swap_copy(t, s, p, held_here).wait_recv()

            @pl.when((core == 0) | receives(s))
            def _():
                swap_copy(t, s, p, held_here).wait_send()

    def halo_sent(s, p):
        for t in range(2):

            @pl.when((col_at == 0) | sends_far(s))
            def _():
                halo_copy(t, s, p, True).wait_send()

        @pl.when(relays_far(s))
        def _():
            relay_copy(0, s, p).wait_send()

    def whole(ref, m):
        return ref[m].reshape(n * r, depth)

    def columns_of(ref):
        rate_rows[...] = jnp.zeros_like(rate_rows)
        for s in range(stretches):
            for m in range(3):
                rate_rows[s, pl.ds(m, 1), :] = ref[m, pl.ds(s, 1), :]
        return [jnp.transpose(rate_rows[s]) for s in range(stretches)]

    def hidden(ref, s, part, rates):
        at = far_rows if part else own_rows
        k, v = kb[s, at], vb[s, at]
        gate_in = mm(k, whole(ref, 0), NT)
        up_in = mm(k, whole(ref, 1), NT)
        back_in = mm(v, whole(ref, 2), NT)
        act, slope = activation(gate_in)
        xs[0, at] = (rates[:, 0:1] * (-back_in * up_in * slope)).astype(bf)
        xs[1, at] = (rates[:, 1:2] * (-back_in * act)).astype(bf)
        xs[2, at] = (rates[:, 2:3] * -(act * up_in)).astype(bf)

    def grads(phase):
        copies = []
        for m in range(3):
            other_side = vb[phase] if m == 2 else kb[phase]
            gp[m] = mm(xs[m], other_side, TN).astype(bf).reshape(n, r, depth)
            copies.append(
                run(gp.at[m, pl.ds((1 - core) * teams, teams)], pair.at[phase, m], partner)
            )
        return copies

    def both(phase, m, g):
        return gp[m, slot_of(g)].astype(f32) + pair[phase, m, g].astype(f32)

    def forward(ref, s, part):
        q = qb[s, far_rows if part else own_rows]
        act, _ = activation(mm(q, whole(ref, 0), NT))
        inner = (act * mm(q, whole(ref, 1), NT)).astype(bf)
        out = mm(inner, whole(ref, 2), NN).astype(bf)
        if not part:
            fast[s, :, cols_of(row_at)] = out
            return None
        back[s] = out
        return run(back.at[s], fast.at[s, :, cols_of(row_at)], to_y)

    def attention(s, p):
        base = s * (rows * n) + me * rows
        places = [s] + [jnp.where(me < b, max(s - 1, 0), s) for b in (1, 2)]
        row = lax.broadcasted_iota(jnp.int32, (rows, rows), 0)
        col = lax.broadcasted_iota(jnp.int32, (rows, rows), 1)
        oks = []
        for behind in range(3):
            gap = row - col + behind * rows
            oks.append((gap >= 0) & (gap < WINDOW) & (col >= behind * rows - base))

        @pl.loop(p * (depth // AD), (p + 1) * (depth // AD))
        def _(h):
            cols = pl.ds(pl.multiple_of(h * AD, AD), AD)
            keys = [akb[s, :, cols], near[0, places[1], :, cols], far[0, places[2], :, cols]]
            values = [avb[s, :, cols], near[1, places[1], :, cols], far[1, places[2], :, cols]]
            q = aqb[s, :, cols]
            scores = [
                jnp.where(ok, mm(q, k, NT) / math.sqrt(AD), -1e30) for ok, k in zip(oks, keys)
            ]
            top = functools.reduce(
                jnp.maximum, [jnp.max(x, -1, keepdims=True) for x in scores]
            )
            total, out = 0.0, 0.0
            for x, v in zip(scores, values):
                p = jnp.exp(x - top)
                total = total + jnp.sum(p, -1, keepdims=True)
                out = out + mm(p.astype(bf), v, NN)
            comb[s, :, cols] = (fast[s, :, cols].astype(f32) + out / total).astype(bf)

    def exchange(s, p):
        first_slot = comm.slots(parts)
        chunk = rows // parts
        copies = []
        for step in range(1, parts):
            z = lax.rem(mine + step, parts)
            take = pl.ds(pl.multiple_of(z * chunk, chunk), chunk)
            copy = comm.make(
                first_slot + step,
                comb.at[s, take, part_of(p)],
                land.at[s, step, :, part_of(p)],
                {"ba": z},
            )
            copy.start()
            copies.append(copy)
        return copies

    def finish(s, copies):
        chunk = rows // parts
        take = pl.ds(pl.multiple_of(mine * chunk, chunk), chunk)
        land[s, 0] = comb[s, take]
        for copy in copies:
            copy.wait()
        squares = 0.0
        for step in range(parts):
            x = land[s, step].astype(f32)
            squares = squares + jnp.sum(x * x, -1, keepdims=True)
        scale = lax.rsqrt(squares / (parts * width) + EPS)
        for step in range(parts):
            z = lax.rem(mine + parts - step, parts)
            cols = pl.ds(pl.multiple_of(z * width, 128), width)
            x = land[s, step].astype(f32)
            mixed[s, :, cols] = (x * scale * gain[:, cols]).astype(bf)

    def renorm(m):
        before, after = 0.0, 0.0
        for j in range(n):
            w = first[m, j].astype(f32)
            t = w - second[m, j].astype(f32)
            before = before + jnp.sum(w * w, 0, keepdims=True)
            after = after + jnp.sum(t * t, 0, keepdims=True)
        target = jnp.sqrt(before + EPS)
        goal[m] = target
        ratio = target / jnp.sqrt(after + EPS)
        for b, g in enumerate((group, above)):
            grad = second[m, slot_of(g)].astype(f32)
            past[b, m] = BETA * grad
            held_w[b, m] = (first[m, slot_of(g)].astype(f32) - grad) * ratio
        for j in range(n):
            w = first[m, j].astype(f32)
            t = w - second[m, j].astype(f32)
            second[m, j] = (t * ratio).astype(bf)

    here, near_y, near_x = slot_of(group), slot_of(above), slot_of(beside)
    corner = slot_of(across)
    up = run(shard.at[other], first.at[:, here], to_y)
    side = run(shard.at[row_at], first.at[:, here], to_x)
    twins = [run(shard.at[row_at], first.at[:, here], partner)]
    rate_copy = run(rate.at[pl.ds(3 * other, 3)], rate_far, to_y)
    first[:, here] = shard[row_at]
    rates = columns_of(rate.at[pl.ds(3 * row_at, 3)])
    up.wait_recv()
    onward = run(first.at[:, near_y], first.at[:, near_y], to_x)
    twins.append(run(first.at[:, near_y], first.at[:, near_y], partner))
    send_tokens("k", 0)
    send_tokens("v", 0)
    side.wait_recv()
    twins.append(run(first.at[:, near_x], first.at[:, near_x], partner))
    for p in range(heads):
        halo(0, p)
    onward.wait_recv()
    twins.append(run(first.at[:, corner], first.at[:, corner], partner))
    for copy in twins:
        copy.wait_recv()

    local["k", 0].wait()
    local["v", 0].wait()
    hidden(first, 0, 0, rates[0])
    rate_copy.wait_recv()
    far_rates = columns_of(rate_far)
    local["q", 0].wait()
    forward(first, 0, 0)
    sent["k", 0].wait_recv()
    sent["v", 0].wait_recv()
    send_tokens("q", 0)
    hidden(first, 0, 1, far_rates[0])
    pairs = grads(0)
    crossing = []
    for m in range(3):
        pairs[m].wait_recv()
        for g in range(teams):
            sums[m, g] = both(0, m, g).astype(bf)
        crossing.append(run(sums.at[m], landed.at[m], to_x))
    send_tokens("k", 1)
    send_tokens("v", 1)
    sent["q", 0].wait_recv()
    send_tokens("q", 1)
    arriving = forward(first, 0, 1)
    for p in range(heads):
        halo_relay(0, p)
    halo(1, 0)
    half = pl.ds(core * teams, teams)
    twins = []
    for m in range(3):
        crossing[m].wait_recv()
        second[m, half] = (sums[m].astype(f32) + landed[m].astype(f32)).astype(bf)
        twins.append(run(second.at[m, half], second.at[m, half], partner))
    halo(1, 1)
    for m in range(3):
        twins[m].wait_recv()
        drained(twins[m])
        drained(pairs[m])
        renorm(m)
    for name in "kv":
        local[name, 1].wait()
        sent[name, 1].wait_recv()
    hidden(second, 1, 0, rates[1])
    hidden(second, 1, 1, far_rates[1])
    pairs = grads(1)
    crossing = []
    for m in range(3):
        pairs[m].wait_recv()
        for k in range(2):
            last_sums[m, k] = both(1, m, k * 2 + 1 - col_at).astype(bf)
        crossing.append(run(last_sums.at[m], last_landed.at[m], to_x))
    sent["q", 1].wait_recv()
    arriving1 = forward(second, 1, 1)
    w_copy = run(second.at[:, near_y], w_far, to_y)
    goal_copy = run(goal, goal_far, to_y)
    local["q", 1].wait()
    forward(second, 1, 0)
    for p in range(heads):
        halo_relay(1, p)
    for name in ("aq", "ak", "av"):
        local[name].wait()
    arriving.wait_recv()
    mixing0 = []
    for p in range(heads):
        halo_swap(0, p)
        attention(0, p)
        mixing0 += exchange(0, p)
    arriving1.wait_recv()
    mixing1 = []
    for p in range(heads):
        halo_swap(1, p)
        attention(1, p)
        mixing1 += exchange(1, p)
    m_copies = []
    for m in range(3):
        crossing[m].wait_recv()
        squares = 0.0
        for b, (g, k) in enumerate(((group, row_at), (above, other))):
            momentum = past[b, m] + both(1, m, g) + last_landed[m, k].astype(f32)
            trial = held_w[b, m] - momentum
            squares = squares + jnp.sum(trial * trial, 0, keepdims=True)
            if b:
                m_out[m] = momentum.astype(bf)
            else:
                moment[row_at, m] = momentum
                weights[row_at, m] = trial
        m_copies.append(run(m_out.at[m], m_far.at[m], to_y))
        sq[me, m] = squares
    first_slot = comm.slots(n)
    copies = []
    for step in range(1, n):
        copy = comm.make(
            first_slot + step, sq.at[me], sq.at[me], {"aa": lax.rem(me + step, n)}
        )
        copy.start()
        copies.append(copy)
    finish(0, mixing0)
    for copy in copies:
        copy.wait()
    w_copy.wait_recv()
    goal_copy.wait_recv()
    for m in range(3):
        m_copies[m].wait_recv()
        squares, squares_far = 0.0, 0.0
        for j in range(teams):
            squares = squares + sq[row_at * teams + j, m]
            squares_far = squares_far + sq[other * teams + j, m]
        weights[row_at, m] = weights[row_at, m] * (goal[m] / jnp.sqrt(squares + EPS))
        momentum = m_far[m].astype(f32)
        moment[other, m] = momentum
        weights[other, m] = (w_far[m].astype(f32) - momentum) * (
            goal_far[m] / jnp.sqrt(squares_far + EPS)
        )
    finish(1, mixing1)
    for copy in tail:
        copy.wait_send()
    for s in range(stretches):
        for p in range(heads):
            halo_sent(s, p)


def run_blocks(fq, fk, fv, rates, aq, ak, av, shard, gain):
    n, parts = lax.axis_size("aa"), lax.axis_size("ba")
    stretches, rows, width = fq.shape
    heads, _, r, depth = shard.shape
    teams = n // 2
    vmem = pl.BlockSpec(memory_space=pltpu.VMEM)
    hbm = pl.BlockSpec(memory_space=pl.ANY)
    piece = (r, depth)
    bf, f32 = jnp.bfloat16, jnp.float32
    slots = 5 * stretches * heads + 2 * heads * parts + n + 64
    token = pltpu.VMEM((stretches, 2 * rows, depth), bf)
    features = pltpu.VMEM((stretches, rows, width), bf)
    return pl.pallas_call(
        functools.partial(block_kernel, n, parts),
        in_specs=[hbm] * 3 + [vmem] + [hbm] * 3 + [vmem] * 2,
        out_specs=(vmem,) * 3,
        out_shape=(
            jax.ShapeDtypeStruct((stretches, rows // parts, width * parts), bf),
            jax.ShapeDtypeStruct((heads, 3) + piece, f32),
            jax.ShapeDtypeStruct((heads, 3) + piece, f32),
        ),
        scratch_shapes=[
            pltpu.VMEM((3, n) + piece, bf),
            pltpu.VMEM((3, n) + piece, bf),
            pltpu.VMEM((3, n) + piece, bf),
            pltpu.VMEM((2, 3, teams) + piece, bf),
            pltpu.VMEM((3, teams) + piece, bf),
            pltpu.VMEM((3, teams) + piece, bf),
            pltpu.VMEM((3, 2) + piece, bf),
            pltpu.VMEM((3, 2) + piece, bf),
            token,
            token,
            token,
            pltpu.VMEM((3, 2 * rows, depth), bf),
            pltpu.VMEM((stretches, 8, rows), f32),
            pltpu.VMEM((3, stretches, rows), f32),
            features,
            features,
            features,
            pltpu.VMEM((2, stretches, rows, width), bf),
            pltpu.VMEM((2, stretches, rows, width), bf),
            features,
            features,
            pltpu.VMEM((stretches, rows, depth), bf),
            features,
            pltpu.VMEM((stretches, parts, rows // parts, width), bf),
            pltpu.VMEM((2, 3) + piece, f32),
            pltpu.VMEM((2, 3) + piece, f32),
            pltpu.VMEM((3, 1, depth), f32),
            pltpu.VMEM((3, 1, depth), f32),
            pltpu.VMEM((3,) + piece, bf),
            pltpu.VMEM((3,) + piece, bf),
            pltpu.VMEM((3,) + piece, bf),
            pltpu.VMEM((n, 3, 1, depth), f32),
            pltpu.SemaphoreType.DMA((3 * stretches + 3,)),
            pltpu.SemaphoreType.DMA((slots,)),
            pltpu.SemaphoreType.DMA((slots,)),
        ],
        compiler_params=pltpu.CompilerParams(
            collective_id=2, has_side_effects=True, vmem_limit_bytes=51 * 2**20
        ),
        name="blocks",
    )(fq, fk, fv, rates, aq, ak, av, shard, gain)


def local_blocks(fq, fk, fv, rates, aq, ak, av, fast_weights, gain):
    shard = jnp.transpose(fast_weights.astype(jnp.bfloat16), (2, 1, 0, 3))
    rate = jnp.transpose(rates, (2, 0, 1))
    mixed, weights, moment = run_blocks(fq, fk, fv, rate, aq, ak, av, shard, gain[None])
    back = (2, 1, 0, 3)
    return (mixed, jnp.transpose(weights, back), jnp.transpose(moment, back))


def pick(*args):
    stretches, rows, _ = args[0].shape
    r, _, heads, depth = args[7].shape
    n, parts = lax.axis_size("aa"), lax.axis_size("ba")
    fits = r % 16 == 0 and n == 8 and depth % AD == 0 and stretches == 2 and heads == 2
    fits = fits and 2 * rows == WINDOW and rows % (16 * parts) == 0
    return (local_blocks if fits else local)(*args)


def solution(mesh):
    token = P(None, "aa", "ba")
    hidden = P("aa", None, "ba", None)
    return jax.shard_map(
        pick,
        mesh=mesh,
        in_specs=(token,) * 7 + (hidden, P()),
        out_specs=(P(None, ("aa", "ba"), None), hidden, hidden),
        check_vma=False,
    )
```
